32 devices in a mesh: bond: 16 (over z, y, x), op: 2 (over core).
Axes of the slice: x: 2, y: 2, z: 4, core: 2. Of those that a mesh axis runs over, the one named last changes fastest.
Arguments:
- wavefunction: float32 [6, 256, 8192], P(None, None, 'bond'), may hold values from -6 to 6
- left_tiles: bfloat16 [16, 16, 2, 128, 128], P('op', None, None, 'bond'), may hold values from -0.375 to 0.375
- right_tiles: bfloat16 [16, 16, 2, 128, 128], P('op', None, None, 'bond'), may hold values from -0.375 to 0.375
- site_operators: float32 [16, 4, 4], P('op'), may hold values from -1.75 to 1.75
- left_charge: int32 [16], replicated, may hold values from 0 to 7, as said below
- right_charge: int32 [16], replicated, may hold values from 0 to 7, as said below
- channel_charge: int32 [16, 2], replicated, may hold values from -1 to 7, as said below
Outputs:
- sigma_one: float32 [6, 256, 8192], P(None, 'bond', 'op')
- sigma_two: float32 [6, 256, 8192], P(None, 'op', 'bond')
The draws below stay inside these ranges and needn't reach their ends.
Inputs may be any that keep to these rules, and one draw needn't show every extreme that they name: `left_charge`: each charge labels exactly 2 of the left blocks. `right_charge`: each charge labels exactly 2 of the right blocks. `channel_charge`: column 0 is a left charge shift, each of 0 to 7 used by exactly 2 channels; column 1 is a site charge shift, each of -1, 0 and 1 used by 5 or 6 channels.
All inputs are finite; a program needn't handle non-finite values.
Results may differ from the reference program's by a relative error of at most 0.0057.
Values may be sent and summed in bfloat16 or wider, within the bound.
A program may use at most 128 MiB of HBM per device.

```python
import jax
import jax.numpy as jnp
from jax import lax

M = 2048
B = 128
NQ = 8
DP = 4
C = 16
K = 6
NB = 16
NPB = 2
NS = 256


def draw_left_charge(key, part):
    ordering = jax.random.permutation(jax.random.fold_in(key, 11), NB)
    return (ordering % NQ).astype(jnp.int32)


def draw_right_charge(key, part):
    ordering = jax.random.permutation(jax.random.fold_in(key, 23), NB)
    return (ordering % NQ).astype(jnp.int32)


def draw_channel_charge(key, part):
    shifts = jax.random.permutation(jax.random.fold_in(key, 31), C) % NQ
    moves = jax.random.permutation(jax.random.fold_in(key, 37), C) % 3 - 1
    return jnp.stack([shifts, moves], axis=1).astype(jnp.int32)


def levels(key, dims, shards, least, top_value):
    def one(axis_at, shards_of):
        heights = jax.random.uniform(jax.random.fold_in(jax.random.fold_in(key, 6), axis_at), (shards_of,), jnp.float32, least / len(shards), top_value / len(shards))
        return jnp.repeat(jnp.exp(heights), dims[axis_at] // shards_of).reshape((-1,) + (1,) * (len(dims) - axis_at - 1))

    level = one(*shards[0])
    for cut in shards[1:]:
        level = level * one(*cut)
    return level


def centred(own_key, dims, deviation, limit, shards=(), held_as=jnp.bfloat16):
    entries = deviation * jax.random.normal(own_key, dims, jnp.float32)
    if shards:
        entries = entries * levels(own_key, dims, shards, -0.22, 0.18)
    return jnp.clip(entries, -limit, limit).astype(held_as)


def setup_inputs(seed: int = 0) -> dict:
    seeds = jax.random.split(jax.random.key(seed), 8)
    return {
        "wavefunction": centred(seeds[0], (K, NS, DP * M), 1.0, 6.0, ((2, 16),), jnp.float32),
        "left_tiles": centred(seeds[1], (C, NB, NPB, B, B), (NPB * B) ** -0.5, 0.375, ((0, 2), (3, 16))),
        "right_tiles": centred(seeds[2], (C, NB, NPB, B, B), (NPB * B) ** -0.5, 0.375, ((0, 2), (3, 16))),
        "site_operators": centred(seeds[3], (C, DP, DP), (3 * DP) ** -0.5, 1.75, ((0, 2),), jnp.float32),
        "left_charge": draw_left_charge(jax.random.fold_in(seeds[7], 71), 0),
        "right_charge": draw_right_charge(jax.random.fold_in(seeds[7], 71), 0),
        "channel_charge": draw_channel_charge(jax.random.fold_in(seeds[7], 71), 0),
    }


site_charge_table = (0, 1, 1, 2)


def block_sources(charge, offset):
    ordering = jnp.argsort(charge, stable=True).astype(jnp.int32)
    target = (charge - offset) % NQ
    slot_index = target[:, None] * NPB + jnp.arange(NPB, dtype=jnp.int32)[None, :]
    return ordering[slot_index]


def site_masks(site_operators, channel_charge):
    site_charge = jnp.array(site_charge_table, dtype=jnp.int32)
    charge_step = site_charge[:, None] - site_charge[None, :]
    allowed = (charge_step[None, :, :] - channel_charge[:, 1][:, None, None]) % NQ == 0
    return jnp.where(allowed, site_operators, jnp.zeros_like(site_operators))


def column_classes(right_charge):
    site_charge = jnp.array(site_charge_table, dtype=jnp.int32)
    starts = jnp.arange(DP * NB, dtype=jnp.int32) * B
    return (site_charge[starts // M] + right_charge[(starts % M) // B]) % NQ


def left_pass(left_set, left_order, row_class, values):
    group_count = row_class.shape[0]
    slots = row_class[:, None] * NPB + jnp.arange(NPB, dtype=jnp.int32)[None, :]
    picked_tiles = left_set[left_order[slots]].astype(jnp.float32)
    blocks = values.reshape(values.shape[0], NPB, B, group_count, B).astype(jnp.float32)
    result = jnp.einsum('gmnab,knbgw->kmagw', picked_tiles, blocks, precision=lax.Precision.HIGHEST)
    return result.reshape(values.shape)


def right_pass(right_set, sources, site_matrix, values):
    root_count = values.shape[0]
    row_count = values.shape[1]
    blocks = values.reshape(root_count, row_count, DP, NB, B)
    picked = blocks[:, :, :, sources].astype(jnp.float32)
    inner_sum = jnp.einsum('jnab,kspjnb->kspja', right_set.astype(jnp.float32), picked,
                           precision=lax.Precision.HIGHEST)
    mixture = jnp.einsum('pq,ksqja->kspja', site_matrix, inner_sum, precision=lax.Precision.HIGHEST)
    return mixture.reshape(values.shape)


def reference(wavefunction, left_tiles, right_tiles, site_operators, left_charge, right_charge, channel_charge):
    sector_psi = lax.optimization_barrier(wavefunction.astype(jnp.bfloat16))
    left_order = jnp.argsort(left_charge, stable=True).astype(jnp.int32)
    classes = column_classes(right_charge)
    right_offsets = -(channel_charge[:, 0] + channel_charge[:, 1])
    right_sources = jax.vmap(block_sources, in_axes=(None, 0))(right_charge, right_offsets)
    site_matrices = site_masks(site_operators, channel_charge)
    channel_items = (left_tiles, right_tiles, right_sources, site_matrices, channel_charge[:, 0])

    def first_pass(running, items):
        left_set, right_set, right_src, site_matrix, shift = items
        row_class = (shift - classes) % NQ
        left_side = lax.optimization_barrier(
            left_pass(left_set, left_order, row_class, sector_psi).astype(jnp.bfloat16))
        return running + right_pass(right_set, right_src, site_matrix, left_side), None

    sigma_one, unused_one = lax.scan(first_pass, jnp.zeros(wavefunction.shape, jnp.float32), channel_items)
    rounded_one = lax.optimization_barrier(sigma_one.astype(jnp.bfloat16))
    second_class = (-classes) % NQ

    def second_pass(running, items):
        left_set, right_set, right_src, site_matrix, shift = items
        right_side = lax.optimization_barrier(
            right_pass(right_set, right_src, site_matrix, rounded_one).astype(jnp.bfloat16))
        return running + left_pass(left_set, left_order, second_class, right_side), None

    sigma_two, unused_two = lax.scan(second_pass, jnp.zeros(wavefunction.shape, jnp.float32), channel_items)
    return sigma_one, sigma_two
```

```python
import functools

import jax
import jax.numpy as jnp
from jax import lax
from jax.experimental import pallas as pl
from jax.experimental.pallas import tpu as pltpu
from jax.sharding import PartitionSpec as P

M = 2048
B = 128
NQ = 8
DP = 4
NB = 16
NPB = 2

site_charge_table = (0, 1, 1, 2)
MESH = pl.DeviceIdType.MESH


def site_masks(site_operators, channel_charge):
    site_charge = jnp.array(site_charge_table, dtype=jnp.int32)
    charge_step = site_charge[:, None] - site_charge[None, :]
    allowed = (charge_step[None, :, :] - channel_charge[:, 1][:, None, None]) % NQ == 0
    return jnp.where(allowed, site_operators, jnp.zeros_like(site_operators))


def spread_kernel(half, ops, colours, first, *refs):
    if first:
        x_ref, y_ref, g_ref = refs[:3]
        z_ref = None
        scratch = refs[3:]
    else:
        x_ref, y_ref, g_ref, z_ref = refs[:4]
        scratch = refs[4:]
    own_sem, psend, precv, send_sem, recv_sem, fsend, frecv = scratch
    bond = lax.axis_index("bond")
    o = lax.axis_index("op")
    i = lax.rem(bond, half)
    part = bond // half
    base = bond - i
    partner = i + half * (1 - part)
    bits = half.bit_length() - 1
    streams = 2 if first else 1

    def place(mask):
        at = i
        for t in range(bits):
            if mask >> t & 1:
                at = at + (1 << t) * (1 - 2 * lax.rem(i // (1 << t), 2))
        return at

    def to(bond_index, op_index):
        return {"bond": bond_index, "op": op_index}

    barrier = pltpu.get_barrier_semaphore()
    for t in range(bits):
        pl.semaphore_signal(
            barrier, inc=1, device_id=to(base + place(1 << t), o), device_id_type=MESH
        )
    pl.semaphore_signal(barrier, inc=1, device_id=to(partner, o), device_id_type=MESH)
    for e in range(1, ops):
        pl.semaphore_signal(
            barrier, inc=1, device_id=to(bond, lax.rem(o + e, ops)), device_id_type=MESH
        )
    pl.semaphore_wait(barrier, bits + ops)

    index = (part, 1 - part) if first else (0,)
    exchange = []
    for c in range(colours if first else 1):
        exchange.append(pltpu.make_async_remote_copy(
            src_ref=y_ref.at[c] if first else y_ref,
            dst_ref=g_ref.at[i, o, part, c] if first else z_ref,
            send_sem=psend.at[c], recv_sem=precv.at[c],
            device_id=to(partner, o), device_id_type=MESH,
        ))
        exchange[-1].start()

    copies = {}
    forwards = []
    ready = set()

    def block(s, c, mask):
        if s == 0 and mask == 0:
            return x_ref.at[c]
        return g_ref.at[place(mask), o, index[s], c]

    def ensure(s, c, mask):
        if (s, c, mask) in ready:
            return
        ready.add((s, c, mask))
        if mask:
            copies[s, c, mask].wait_recv()
        elif s == 1:
            exchange[c].wait_recv()
        for e in range(1, ops):
            copy = pltpu.make_async_remote_copy(
                src_ref=block(s, c, mask), dst_ref=g_ref.at[place(mask), o, index[s], c],
                send_sem=fsend.at[s, c, mask, e], recv_sem=frecv.at[s, c, mask, e],
                device_id=to(bond, lax.rem(o + e, ops)), device_id_type=MESH,
            )
            copy.start()
            forwards.append(copy)

    own = pltpu.make_async_copy(x_ref, g_ref.at[i, o, index[0]], own_sem)
    own.start()
    for s in range(streams):
        reached = [[0] for c in range(colours)]
        for step in range(bits):
            for at in range(max(len(r) for r in reached)):
                for c in range(colours):
                    mask = reached[c][at]
                    bit = 1 << (c + step) % bits
                    ensure(s, c, mask)
                    copy = pltpu.make_async_remote_copy(
                        src_ref=block(s, c, mask), dst_ref=g_ref.at[place(mask), o, index[s], c],
                        send_sem=send_sem.at[s, c, mask | bit], recv_sem=recv_sem.at[s, c, mask | bit],
                        device_id=to(base + place(bit), o), device_id_type=MESH,
                    )
                    copy.start()
                    copies[s, c, mask | bit] = copy
            for c in range(colours):
                bit = 1 << (c + step) % bits
                reached[c] = reached[c] + [mask | bit for mask in reached[c]]
    for s in range(streams):
        for mask in range(half):
            for c in range(colours):
                ensure(s, c, mask)
    own.wait()
    for copy in copies.values():
        copy.wait_send()
    for copy in exchange:
        copy.wait_send()
        if not first:
            copy.wait_recv()
    for copy in forwards:
        copy.wait()


def spread(x, y, half, ops, first):
    colours = x.shape[0]
    streams = 2 if first else 1
    shapes = [jax.ShapeDtypeStruct((half, ops, streams) + x.shape, x.dtype)]
    if not first:
        shapes.append(jax.ShapeDtypeStruct(y.shape, y.dtype))
    size = x.size * half * ops * streams * 2
    return pl.pallas_call(
        functools.partial(spread_kernel, half, ops, colours, first),
        out_shape=shapes,
        in_specs=[pl.BlockSpec(memory_space=pltpu.VMEM)] * 2,
        out_specs=[pl.BlockSpec(memory_space=pl.ANY)] * len(shapes),
        scratch_shapes=[
            pltpu.SemaphoreType.DMA,
            pltpu.SemaphoreType.DMA((colours,)),
            pltpu.SemaphoreType.DMA((colours,)),
            pltpu.SemaphoreType.DMA((streams, colours, half)),
            pltpu.SemaphoreType.DMA((streams, colours, half)),
            pltpu.SemaphoreType.DMA((streams, colours, half, ops)),
            pltpu.SemaphoreType.DMA((streams, colours, half, ops)),
        ],
        compiler_params=pltpu.CompilerParams(
            collective_id=1 if first else 2, has_side_effects=True
        ),
        cost_estimate=pl.CostEstimate(flops=0, bytes_accessed=16 * size, transcendentals=0),
        name="spread_first" if first else "spread_second",
    )(x, y)


def apply_kernel(
    channels, rows, roots, site_charges, load,
    order_ref, shift_ref, site_ref, psi_ref, left_ref, right_ref, out_ref, mixed
):
    @pl.loop(0, NQ)
    def _(g):
        for n in range(NPB):
            r = order_ref[g * NPB + n]
            terms = []
            for q in range(DP):
                h = lax.rem(2 * NQ - site_charges[q] - g, NQ)
                terms.append(
                    jnp.dot(left_ref[h], load(psi_ref, q * NB + r), preferred_element_type=jnp.float32)
                )
            for c in range(channels):
                for p in range(DP):
                    total = site_ref[(c * DP + p) * DP] * terms[0][c * rows:(c + 1) * rows]
                    for q in range(1, DP):
                        total += site_ref[(c * DP + p) * DP + q] * terms[q][c * rows:(c + 1) * rows]
                    total = total.astype(jnp.bfloat16)
                    for k in range(roots):
                        at = (p * roots + k) * rows
                        mixed[c, g, at:at + rows, n * B:(n + 1) * B] = total[:, k * B:(k + 1) * B]

    @pl.loop(0, NQ)
    def _(g):
        total = None
        for c in range(channels):
            source = lax.rem(g + shift_ref[c], NQ)
            term = lax.dot_general(
                mixed[c, source], right_ref[c, g], (((1,), (1,)), ((), ())),
                preferred_element_type=jnp.float32,
            )
            total = term if total is None else total + term
        for m in range(NPB):
            out_ref[order_ref[g * NPB + m]] = total[:, m * B:(m + 1) * B]


def apply_all(order, shift, site, psi, left, right, rows, roots, load):
    channels = right.shape[0]
    height = DP * roots * rows
    smem = pl.BlockSpec(memory_space=pltpu.SMEM)
    vmem = pl.BlockSpec(memory_space=pltpu.VMEM)
    return pl.pallas_call(
        functools.partial(apply_kernel, channels, rows, roots, site_charge_table, load),
        out_shape=jax.ShapeDtypeStruct((NB, height, B), jnp.float32),
        in_specs=[smem, smem, smem, vmem, vmem, vmem],
        out_specs=vmem,
        scratch_shapes=[pltpu.VMEM((channels, NQ, height, NPB * B), jnp.bfloat16)],
        compiler_params=pltpu.CompilerParams(vmem_limit_bytes=58 * 1024 * 1024),
        name="apply_all",
    )(order, shift, site, psi, left, right)


def whole_kernel(
    half, ops, some, channels, site_charges,
    order_ref, rank_ref, left_order_ref, shift_ref, left_shift_ref, site_ref,
    wave_ref, lt_ref, rt_ref, one_ref, two_ref,
    psi, gathered, right, left, left_raw, mixed, part_sum, got_first, got_second, stage, away,
    swap, sorted_out, ready, landed,
    stage_sem, psend, precv, send_sem, recv_sem, fsend, frecv,
    rpsend, rprecv, rsend, rrecv, lsend, lrecv, lown, osend, orecv, osend2, orecv2,
    wsend, wrecv, asend, arecv, free_sem,
):
    bond = lax.axis_index("bond")
    o = lax.axis_index("op")
    bonds = 2 * half
    i = lax.rem(bond, half)
    part = bond // half
    base = bond - i
    partner = i + half * (1 - part)
    bits = half.bit_length() - 1
    rows = left.shape[1] // channels
    sub = rows // NPB
    fine = lt_ref.shape[3]
    streams = 2
    other = lax.rem(o + 1, ops)

    def place(mask):
        at = i
        for t in range(bits):
            if mask >> t & 1:
                at = at + (1 << t) * (1 - 2 * lax.rem(i // (1 << t), 2))
        return at

    def turn(x):
        return lax.rem(2 * x, half) + (2 * x) // half

    def to(bond_index, op_index):
        return {"bond": bond_index, "op": op_index}

    def remote(src, dst, send, recv, bond_index, op_index):
        return pltpu.make_async_remote_copy(
            src_ref=src, dst_ref=dst, send_sem=send, recv_sem=recv,
            device_id=to(bond_index, op_index), device_id_type=MESH,
        )

    barrier = pltpu.get_barrier_semaphore()
    for e in range(1, bonds):
        pl.semaphore_signal(
            barrier, inc=1, device_id=to(lax.rem(bond + e, bonds), o), device_id_type=MESH
        )
    pl.semaphore_signal(barrier, inc=1, device_id=to(bond, other), device_id_type=MESH)

    share = stage.shape[1]
    groups = stage.shape[2] // B
    load = pltpu.make_async_copy(wave_ref.at[:, pl.ds(o * share, share), :], stage, stage_sem)
    load.start()
    load.wait()
    tiles = share // sub
    for k in range(some):
        for at in range(groups):
            for t in range(tiles):
                psi[i, o, k, part, at * tiles + t] = stage[
                    part * some + k, t * sub:(t + 1) * sub, at * B:(at + 1) * B
                ].astype(jnp.bfloat16)
                away[k, at * tiles + t] = stage[
                    (1 - part) * some + k, t * sub:(t + 1) * sub, at * B:(at + 1) * B
                ].astype(jnp.bfloat16)
    pl.semaphore_wait(barrier, bonds)

    def spread(index, exchange):
        colours = some
        copies, forwards, ready_set = {}, [], set()

        def slot(s, c, mask):
            return psi.at[place(mask), o, c, index[s]]

        def ensure(s, c, mask):
            if (s, c, mask) in ready_set:
                return
            ready_set.add((s, c, mask))
            if mask:
                copies[s, c, mask].wait_recv()
            elif s == 1 and exchange:
                exchange[c].wait_recv()
            copy = remote(slot(s, c, mask), slot(s, c, mask), fsend.at[s, c, mask],
                          frecv.at[s, c, mask], bond, other)
            copy.start()
            forwards.append(copy)

        reached = [[[0] for c in range(colours)] for s in range(streams)]

        def step(s, n):
            for at in range(1 << n):
                for c in range(colours):
                    mask = reached[s][c][at]
                    bit = 1 << (c + n) % bits
                    ensure(s, c, mask)
                    copy = remote(slot(s, c, mask), slot(s, c, mask), send_sem.at[s, c, mask | bit],
                                  recv_sem.at[s, c, mask | bit], base + place(bit), o)
                    copy.start()
                    copies[s, c, mask | bit] = copy
            for c in range(colours):
                bit = 1 << (c + n) % bits
                reached[s][c] = reached[s][c] + [mask | bit for mask in reached[s][c]]

        def finish():
            for s in range(streams):
                for mask in range(half):
                    for c in range(colours):
                        ensure(s, c, mask)
            for copy in copies.values():
                copy.wait_send()
            for copy in exchange:
                copy.wait_send()
            for copy in forwards:
                copy.wait()

        return step, finish

    exchange = []
    for c in range(some):
        exchange.append(remote(away.at[c], psi.at[i, o, c, part], psend.at[c], precv.at[c], partner, o))
        exchange[-1].start()
    psi_step, psi_finish = spread((part, 1 - part), exchange)
    psi_step(0, 0)

    @pl.loop(0, channels)
    def _(c):
        for g in range(NQ):
            bands = []
            for m in range(NPB):
                r = order_ref[g * NPB + m]
                bands.append(jnp.concatenate(
                    [rt_ref[c, r, n].astype(jnp.float32) for n in range(NPB)], 1))
            gathered[bond, c, g] = jnp.concatenate(bands, 0).astype(jnp.bfloat16)

    last = bits - 1
    orders = [(last, 0, 1), (last, 1, 0), (0, last, 1), (1, last, 0)]
    paints = len(orders)
    wide = channels // paints

    def tile(slot, c):
        return gathered.at[slot, pl.ds(c * wide, wide)]

    right_exchange = []
    for c in range(paints):
        right_exchange.append(remote(tile(bond, c), tile(bond, c), rpsend.at[c], rprecv.at[c], partner, o))
    right_copies, right_ready = {}, set()

    def right_ensure(s, c, mask):
        if (s, c, mask) in right_ready:
            return
        right_ready.add((s, c, mask))
        if mask:
            right_copies[s, c, mask].wait_recv()
        elif s == 1:
            right_exchange[c].wait_recv()

    right_reached = [[[0] for c in range(paints)] for s in range(streams)]

    def right_step(s, n):
        start = base if s == 0 else half - base
        for at in range(1 << n):
            for c in range(paints):
                mask = right_reached[s][c][at]
                bit = 1 << orders[c][n]
                right_ensure(s, c, mask)
                here = tile(start + place(mask), c)
                copy = remote(here, here, rsend.at[s, c, mask | bit], rrecv.at[s, c, mask | bit],
                              base + place(bit), o)
                copy.start()
                right_copies[s, c, mask | bit] = copy
        for c in range(paints):
            bit = 1 << orders[c][n]
            right_reached[s][c] = right_reached[s][c] + [mask | bit for mask in right_reached[s][c]]

    for copy in right_exchange:
        copy.start()
    parity = lax.rem(bond, 2)
    left_targets = []
    for h in range(2):
        target = h * half + turn(bond // 2)
        left_targets.append((target, remote(
            lt_ref, left_raw.at[parity], lsend.at[h], lrecv.at[parity], target, o)))
    own_left = pltpu.make_async_copy(lt_ref, left_raw.at[parity], lown)
    for target, copy in left_targets:
        @pl.when(target != bond)
        def _():
            copy.start()

        @pl.when(target == bond)
        def _():
            own_left.start()

    right_step(0, 0)
    psi_step(0, 1)
    psi_step(0, 2)
    right_step(0, 1)
    psi_step(1, 0)
    psi_step(1, 1)
    psi_step(1, 2)
    right_step(0, 2)
    right_step(1, 0)
    right_step(1, 1)

    band = i // 2 + lax.rem(i, 2) * (half // 2)
    for t in range(2):
        source = 2 * band + t

        @pl.when(source != bond)
        def _():
            remote(lt_ref, left_raw.at[t], lsend.at[0], lrecv.at[t], source, o).wait_recv()

        @pl.when(source == bond)
        def _():
            own_left.wait()

    @pl.loop(0, NQ)
    def _(h):
        for c in range(channels):
            slot = lax.rem(h + left_shift_ref[c], NQ)
            for m in range(NPB):
                r = left_order_ref[slot * NPB + m]
                pieces = []
                for t in range(2):
                    pieces.append(jnp.concatenate(
                        [left_raw[t, c, r, n].astype(jnp.float32) for n in range(NPB)], 1))
                at = c * rows + m * sub
                left[h, at:at + sub] = jnp.concatenate(pieces, 0).astype(jnp.bfloat16)

    right_step(1, 2)
    psi_finish()

    def left_dots(fetch):
        @pl.loop(0, NQ)
        def _(g):
            for n in range(NPB):
                terms = []
                for q in range(DP):
                    h = lax.rem(2 * NQ - site_charges[q] - g, NQ)
                    terms.append(
                        jnp.dot(left[h], fetch(q, g, n), preferred_element_type=jnp.float32)
                    )
                for c in range(channels):
                    for p in range(DP):
                        total = site_ref[(c * DP + p) * DP] * terms[0][c * rows:(c + 1) * rows]
                        for q in range(1, DP):
                            total += site_ref[(c * DP + p) * DP + q] * terms[q][c * rows:(c + 1) * rows]
                        total = total.astype(jnp.bfloat16)
                        for k in range(some):
                            at = (p * some + k) * rows
                            mixed[c, g, at:at + rows, n * B:(n + 1) * B] = total[:, k * B:(k + 1) * B]

    def fetch_first(q, g, n):
        r = order_ref[g * NPB + n]
        owner = q * (NB // groups) + r // groups
        at = lax.rem(r, groups)
        t, j = owner // half, lax.rem(owner, half)
        return jnp.concatenate([
            jnp.concatenate([
                psi[j, e, k, t, pl.ds(at * tiles, tiles)].reshape(share, B) for e in range(ops)
            ], 0) for k in range(some)
        ], 1)

    left_dots(fetch_first)
    for t in range(bits):
        pl.semaphore_signal(free_sem, inc=1, device_id=to(base + place(1 << t), o), device_id_type=MESH)
    pl.semaphore_signal(free_sem, inc=1, device_id=to(bond, other), device_id_type=MESH)

    for s in range(streams):
        for c in range(paints):
            for mask in range(half):
                right_ensure(s, c, mask)
    for copy in right_exchange:
        copy.wait_send()
    for copy in right_copies.values():
        copy.wait_send()
    for target, copy in left_targets:
        @pl.when(target != bond)
        def _():
            copy.wait_send()

    def right_dots(g):
        total = None
        for c in range(channels):
            source = lax.rem(g + shift_ref[c], NQ)
            term = lax.dot_general(
                mixed[c, source], right[c, g], (((1,), (1,)), ((), ())),
                preferred_element_type=jnp.float32,
            )
            total = term if total is None else total + term
        return total

    own_half = DP // ops * some * rows

    @pl.loop(0, NQ)
    def _(g):
        for c in range(channels):
            for u in range(bonds // 2):
                pair = [gathered[2 * u + t, c, g].astype(jnp.float32) for t in range(2)]
                for m in range(NPB):
                    at = m * B + u * sub
                    right[c, g, at:at + sub] = jnp.concatenate(
                        [x[m * fine:(m + 1) * fine] for x in pair], 0).astype(jnp.bfloat16)
        total = right_dots(g)
        for e in range(ops):
            part_sum[g, e] = total[e * own_half:(e + 1) * own_half]
        remote(part_sum.at[g, other], got_first.at[g], osend.at[g], orecv.at[g], bond, other).start()

    pl.semaphore_wait(free_sem, bits + 1)

    @pl.loop(0, NQ)
    def _(g):
        remote(part_sum.at[g, other], got_first.at[g], osend.at[g], orecv.at[g], bond, other).wait()
        total = (part_sum[g, o] + got_first[g]).astype(jnp.bfloat16)
        for p in range(DP // ops):
            for k in range(some):
                for m in range(NPB):
                    at = ((p * some + k) * NPB + m) * sub
                    for n in range(NPB):
                        psi[i, o, k, p, m * NB + g * NPB + n] = total[at:at + sub, n * B:(n + 1) * B]

    again_step, again_finish = spread((0, 1), [])
    again_step(0, 0)
    again_step(1, 0)
    for n in range(1, bits):
        again_step(0, n)
        again_step(1, n)
    again_finish()

    holder = turn(i)
    wanted = psi.at[holder, o, :, :, pl.ds((1 - part) * NB, NB)]
    trade = remote(wanted, swap, wsend, wrecv, partner, o)
    trade.start()

    def slot_of(x):
        return lax.rem(2 * x, half) + (2 * x) // half if not isinstance(x, int) else (2 * x) % half + (2 * x) // half

    def fetch_second(q, g, n):
        per = DP // ops
        return jnp.concatenate([
            jnp.concatenate([
                psi[slot_of(x), q // per, k, q % per, m * NB + g * NPB + n]
                for m in range(NPB) for x in range(half)
            ], 0) for k in range(some)
        ], 1)

    left_dots(fetch_second)

    @pl.loop(0, NQ)
    def _(g):
        total = right_dots(g)
        for x in range(DP * some):
            for m in range(NPB):
                at = x * rows + m * sub
                part_sum[g, m, x * sub:(x + 1) * sub] = total[at:at + sub]
        remote(part_sum.at[g, other], got_second.at[g], osend2.at[g], orecv2.at[g], bond, other).start()

    @pl.loop(0, NQ)
    def _(g):
        remote(part_sum.at[g, other], got_second.at[g], osend2.at[g], orecv2.at[g], bond, other).wait()
        total = (part_sum[g, o] + got_second[g]).astype(jnp.bfloat16)
        for n in range(NPB):
            for x in range(DP * some):
                sorted_out[g * NPB + n, x] = total[x * sub:(x + 1) * sub, n * B:(n + 1) * B]

    for r in range(NB):
        s = rank_ref[r]
        for p in range(DP):
            for k in range(some):
                ready[p * (NB // groups) + r // groups, k, r % groups] = sorted_out[s, p * some + k]

    sends = []
    for e in range(1, bonds):
        target = lax.rem(bond + e, bonds)
        copy = remote(ready.at[target], landed.at[bond], asend.at[e], arecv.at[e], target, o)
        copy.start()
        sends.append(copy)

    trade.wait()
    for p in range(DP // ops):
        for r in range(NB):
            s = rank_ref[r]
            for k in range(some):
                cols = slice((p * NB + r) * B, (p * NB + r + 1) * B)
                one_ref[part * some + k, :, cols] = psi[
                    holder, o, k, p, part * NB + s].astype(jnp.float32)
                one_ref[(1 - part) * some + k, :, cols] = swap[k, p, s].astype(jnp.float32)

    landed[bond] = ready[bond]
    for copy in sends:
        copy.wait()
    for s in range(bonds):
        x = s % half
        spot = x // 2 + (x % 2) * (half // 2)
        for k in range(some):
            for at in range(groups):
                two_ref[(s // half) * some + k, spot * sub:(spot + 1) * sub, at * B:(at + 1) * B] = (
                    landed[s, k, at].astype(jnp.float32))


def whole(wave, left_tiles, right_tiles, tables, bonds, ops):
    roots, sector_rows, strip = wave.shape
    channels = left_tiles.shape[0]
    half = bonds // 2
    bits = half.bit_length() - 1
    some = roots // 2
    fine = left_tiles.shape[3]
    sub = 2 * fine
    rows = NPB * sub
    share = sector_rows // ops
    groups = strip // B
    height = DP * some * rows
    paints = 4
    vmem = pl.BlockSpec(memory_space=pltpu.VMEM)
    smem = pl.BlockSpec(memory_space=pltpu.SMEM)
    dma = pltpu.SemaphoreType.DMA
    bf, f32 = jnp.bfloat16, jnp.float32
    return pl.pallas_call(
        functools.partial(whole_kernel, half, ops, some, channels, site_charge_table),
        out_shape=[
            jax.ShapeDtypeStruct((roots, NPB * B // bonds, DP // ops * NB * B), f32),
            jax.ShapeDtypeStruct((roots, share, strip), f32),
        ],
        in_specs=[smem] * 6 + [pl.BlockSpec(memory_space=pl.ANY), vmem, vmem],
        out_specs=[vmem, vmem],
        scratch_shapes=[
            pltpu.VMEM((half, ops, some, 2, groups * share // sub, sub, B), bf),
            pltpu.VMEM((bonds, channels, NQ, NPB * fine, NPB * B), bf),
            pltpu.VMEM((channels, NQ, NPB * B, NPB * B), bf),
            pltpu.VMEM((NQ, channels * rows, NPB * B), bf),
            pltpu.VMEM((2,) + left_tiles.shape, bf),
            pltpu.VMEM((channels, NQ, height, NPB * B), bf),
            pltpu.VMEM((NQ, ops, height // ops, NPB * B), f32),
            pltpu.VMEM((NQ, height // ops, NPB * B), f32),
            pltpu.VMEM((NQ, height // ops, NPB * B), f32),
            pltpu.VMEM((roots, share, strip), f32),
            pltpu.VMEM((some, groups * share // sub, sub, B), bf),
            pltpu.VMEM((some, DP // ops, NB, sub, B), bf),
            pltpu.VMEM((NB, DP * some, sub, B), bf),
            pltpu.VMEM((bonds, some, groups, sub, B), bf),
            pltpu.VMEM((bonds, some, groups, sub, B), bf),
            dma, dma((some,)), dma((some,)),
            dma((2, some, half)), dma((2, some, half)), dma((2, some, half)), dma((2, some, half)),
            dma((paints,)), dma((paints,)), dma((2, paints, half)), dma((2, paints, half)),
            dma((2,)), dma((2,)), dma,
            dma((NQ,)), dma((NQ,)), dma((NQ,)), dma((NQ,)),
            dma, dma, dma((bonds,)), dma((bonds,)),
            pltpu.SemaphoreType.REGULAR,
        ],
        compiler_params=pltpu.CompilerParams(
            collective_id=3, has_side_effects=True, vmem_limit_bytes=67043328
        ),
        name="whole",
    )(*tables, wave, left_tiles, right_tiles)


def ordering(charge):
    at = jnp.arange(charge.shape[-1], dtype=jnp.int32)
    mine, theirs = charge[..., :, None], charge[..., None, :]
    before = (theirs < mine) | ((theirs == mine) & (at[None, :] < at[:, None]))
    rank = jnp.sum(before.astype(jnp.int32), -1)
    order = jnp.sum(jnp.where(rank[..., None, :] == at[:, None], at[None, :], 0), -1)
    return order, rank


def local_whole(
    wavefunction, left_tiles, right_tiles, site_operators, left_charge, right_charge, channel_charge
):
    channels = site_operators.shape[0]
    op = lax.axis_index("op")
    own_charge = lax.dynamic_slice_in_dim(channel_charge, op * channels, channels, 0)
    left_order, unused = ordering(left_charge)
    right_order, right_rank = ordering(right_charge)
    shift = (own_charge[:, 0] + own_charge[:, 1] + NQ) % NQ
    site = site_masks(site_operators, own_charge).reshape(-1)
    tables = (right_order, right_rank, left_order, shift, own_charge[:, 0] % NQ, site)
    return tuple(whole(
        wavefunction, left_tiles, right_tiles, tables, lax.axis_size("bond"), lax.axis_size("op")
    ))


def fits(mesh, wavefunction, left_tiles):
    bonds, ops = mesh.shape["bond"], mesh.shape["op"]
    strip = wavefunction.shape[2] // bonds
    fine = left_tiles.shape[3] // bonds
    channels = left_tiles.shape[0] // ops
    return (
        ops == NPB and bonds == NB and strip % B == 0 and 2 * fine * (bonds // 2) == B
        and channels % 4 == 0 and NPB * fine == 16
    )


def local(
    wavefunction, left_tiles, right_tiles, site_operators, left_charge, right_charge, channel_charge
):
    bonds = lax.axis_size("bond")
    ops = lax.axis_size("op")
    bond = lax.axis_index("bond")
    op = lax.axis_index("op")
    roots, sector_rows, strip = wavefunction.shape
    channels = site_operators.shape[0]
    half = bonds // 2
    part = bond // half
    some = roots // 2
    chunk = left_tiles.shape[3]
    band = 2 * chunk
    rows = NPB * band
    held = -(-rows // 16) * 16
    width = min(strip, B)
    groups = strip // width
    own_charge = lax.dynamic_slice_in_dim(channel_charge, op * channels, channels, 0)
    left_order = jnp.argsort(left_charge, stable=True).astype(jnp.int32)
    right_order = jnp.argsort(right_charge, stable=True).astype(jnp.int32)
    shift = (own_charge[:, 0] + own_charge[:, 1]) % NQ
    site = site_masks(site_operators, own_charge).reshape(-1)

    right = right_tiles[:, right_order].transpose(0, 1, 3, 2, 4).reshape(
        channels, NB, chunk, NPB * B
    )
    right = lax.all_gather(right, "bond", axis=2, tiled=True).reshape(
        channels, NQ, NPB * B, NPB * B
    )

    even = [(b, b // 2 + (b % 2) * half) for b in range(bonds)]
    odd = [(b, b // 2 + (1 - b % 2) * half) for b in range(bonds)]
    one = lax.ppermute(left_tiles, "bond", even)
    two = lax.ppermute(left_tiles, "bond", odd)
    low = jnp.where(part == 0, one, two)
    high = jnp.where(part == 0, two, one)
    left = jnp.concatenate([low, high], axis=3)
    left_slots = ((jnp.arange(NQ)[:, None] + own_charge[None, :, 0]) % NQ)[:, :, None] * NPB + jnp.arange(NPB)
    left = left[jnp.arange(channels)[None, :, None], left_order[left_slots]]
    left = left.transpose(0, 1, 2, 4, 3, 5).reshape(NQ, channels, rows, NPB * B)
    left = jnp.pad(left, ((0, 0), (0, 0), (0, held - rows), (0, 0)))
    left = left.reshape(NQ, channels * held, NPB * B)

    share = sector_rows // ops
    psi = lax.dynamic_slice_in_dim(wavefunction, op * share, share, 1).astype(jnp.bfloat16)
    psi = psi.reshape(2, some, share, groups, width).transpose(0, 1, 3, 2, 4)
    kept = lax.dynamic_index_in_dim(psi, part, 0, keepdims=False)
    other = lax.dynamic_index_in_dim(psi, 1 - part, 0, keepdims=False)
    (psi,) = spread(kept, other, half, ops, True)

    def load_whole(ref, block):
        return ref[block]

    def load_first(ref, block):
        owner = block // groups
        t, j, at = owner // half, lax.rem(owner, half), lax.rem(block, groups)
        return jnp.concatenate(
            [jnp.concatenate([ref[j, o, t, k, at] for o in range(ops)], 0) for k in range(some)], 1
        )

    load = load_first
    if width < B:
        psi = psi.reshape(half, ops, 2, some, share, strip).transpose(2, 0, 5, 1, 4, 3)
        psi = psi.reshape(DP * NB, B, sector_rows, some).transpose(0, 2, 3, 1)
        psi = psi.reshape(DP * NB, sector_rows, some * B)
        load = load_whole
    elif share % 16:
        psi = psi.transpose(2, 0, 4, 1, 5, 3, 6).reshape(DP * NB, sector_rows, some * B)
        load = load_whole

    def unpack(result):
        result = result.reshape(NB, DP, some, held, B)[:, :, :, :rows]
        return result.reshape(NB, DP, some, NPB, band, B)

    def summed_share(parts, axis):
        size = parts.shape[axis] // ops
        total = lax.dynamic_slice_in_dim(parts, op * size, size, axis)
        for e in range(1, ops):
            to = (op + e) % ops
            sent = lax.dynamic_slice_in_dim(parts, to * size, size, axis)
            total += lax.ppermute(sent, "op", [(o, (o + e) % ops) for o in range(ops)])
        return total

    first = unpack(apply_all(right_order, shift, site, psi, left, right, held, some, load))
    turned = (DP * NB, some, NPB, band, B)
    if DP % ops == 0:
        first = summed_share(first, 1).transpose(1, 0, 2, 3, 4, 5)
        first = first.reshape((DP * NB // ops,) + turned[1:])
    else:
        first = summed_share(first.transpose(1, 0, 2, 3, 4, 5).reshape(turned), 0)
    blocks = first.shape[0]

    mine = lax.dynamic_index_in_dim(first, part, 2, keepdims=False)
    theirs = lax.dynamic_index_in_dim(first, 1 - part, 2, keepdims=False)
    again = first.astype(jnp.bfloat16).transpose(1, 0, 2, 3, 4)
    again, back = spread(again, theirs.astype(jnp.bfloat16), half, ops, False)
    back = back.astype(jnp.float32)
    both = jnp.stack([jnp.where(part == 0, mine, back), jnp.where(part == 0, back, mine)])
    sigma_one = both.transpose(0, 2, 3, 1, 4).reshape(roots, band, blocks * B)

    def load_second(ref, block):
        o, at = block // blocks, lax.rem(block, blocks)
        return jnp.concatenate(
            [
                jnp.concatenate([ref[j, o, 0, k, at, m] for m in range(NPB) for j in range(half)], 0)
                for k in range(some)
            ], 1,
        )

    load = load_second
    if band % 16:
        again = again[:, :, 0].transpose(1, 3, 4, 0, 5, 2, 6)
        again = again.reshape(DP * NB, sector_rows, some * B)
        load = load_whole
    second = unpack(apply_all(right_order, shift, site, again, left, right, held, some, load))
    if ops == NPB:
        second = summed_share(second, 3)
    else:
        second = lax.psum(second, "op")
    tiles = second.shape[3]
    second = second.astype(jnp.bfloat16).transpose(2, 3, 4, 1, 0, 5)
    second = second.reshape(some, tiles * band, bonds, strip).transpose(2, 0, 1, 3)
    second = lax.all_to_all(second, "bond", split_axis=0, concat_axis=0, tiled=True)
    second = second.reshape(2, half, some, tiles, band, strip).transpose(0, 2, 3, 1, 4, 5)
    second = second.reshape(roots, tiles * B, strip).astype(jnp.float32)
    if ops != NPB:
        second = lax.dynamic_slice_in_dim(second, op * share, share, 1)
    return (sigma_one, second)


def solution(mesh):
    def run(*args):
        body = local_whole if fits(mesh, args[0], args[1]) else local
        return jax.shard_map(
            body,
            mesh=mesh,
            in_specs=(
                P(None, None, "bond"),
                P("op", None, None, "bond", None),
                P("op", None, None, "bond", None),
                P("op", None, None),
                P(),
                P(),
                P(),
            ),
            out_specs=(P(None, "bond", "op"), P(None, "op", "bond")),
            check_vma=False,
        )(*args)

    return run
```

```python
import functools

import jax
import jax.numpy as jnp
from jax import lax
from jax.experimental import pallas as pl
from jax.experimental.pallas import tpu as pltpu
from jax.sharding import PartitionSpec as P

M = 2048
B = 128
NQ = 8
DP = 4
NB = 16
NPB = 2

site_charge_table = (0, 1, 1, 2)
MESH = pl.DeviceIdType.MESH


def site_masks(site_operators, channel_charge):
    site_charge = jnp.array(site_charge_table, dtype=jnp.int32)
    charge_step = site_charge[:, None] - site_charge[None, :]
    allowed = (charge_step[None, :, :] - channel_charge[:, 1][:, None, None]) % NQ == 0
    return jnp.where(allowed, site_operators, jnp.zeros_like(site_operators))


def spread_kernel(half, ops, colours, first, *refs):
    if first:
        x_ref, y_ref, g_ref = refs[:3]
        z_ref = None
        scratch = refs[3:]
    else:
        x_ref, y_ref, g_ref, z_ref = refs[:4]
        scratch = refs[4:]
    own_sem, psend, precv, send_sem, recv_sem, fsend, frecv = scratch
    bond = lax.axis_index("bond")
    o = lax.axis_index("op")
    i = lax.rem(bond, half)
    part = bond // half
    base = bond - i
    partner = i + half * (1 - part)
    bits = half.bit_length() - 1
    streams = 2 if first else 1

    def place(mask):
        at = i
        for t in range(bits):
            if mask >> t & 1:
                at = at + (1 << t) * (1 - 2 * lax.rem(i // (1 << t), 2))
        return at

    def to(bond_index, op_index):
        return {"bond": bond_index, "op": op_index}

    barrier = pltpu.get_barrier_semaphore()
    for t in range(bits):
        pl.semaphore_signal(
            barrier, inc=1, device_id=to(base + place(1 << t), o), device_id_type=MESH
        )
    pl.semaphore_signal(barrier, inc=1, device_id=to(partner, o), device_id_type=MESH)
    for e in range(1, ops):
        pl.semaphore_signal(
            barrier, inc=1, device_id=to(bond, lax.rem(o + e, ops)), device_id_type=MESH
        )
    pl.semaphore_wait(barrier, bits + ops)

    index = (part, 1 - part) if first else (0,)
    exchange = []
    for c in range(colours if first else 1):
        exchange.append(pltpu.make_async_remote_copy(
            src_ref=y_ref.at[c] if first else y_ref,
            dst_ref=g_ref.at[i, o, part, c] if first else z_ref,
            send_sem=psend.at[c], recv_sem=precv.at[c],
            device_id=to(partner, o), device_id_type=MESH,
        ))
        exchange[-1].start()

    copies = {}
    forwards = []
    ready = set()

    def block(s, c, mask):
        if s == 0 and mask == 0:
            return x_ref.at[c]
        return g_ref.at[place(mask), o, index[s], c]

    def ensure(s, c, mask):
        if (s, c, mask) in ready:
            return
        ready.add((s, c, mask))
        if mask:
            copies[s, c, mask].wait_recv()
        elif s == 1:
            exchange[c].wait_recv()
        for e in range(1, ops):
            copy = pltpu.make_async_remote_copy(
                src_ref=block(s, c, mask), dst_ref=g_ref.at[place(mask), o, index[s], c],
                send_sem=fsend.at[s, c, mask, e], recv_sem=frecv.at[s, c, mask, e],
                device_id=to(bond, lax.rem(o + e, ops)), device_id_type=MESH,
            )
            copy.start()
            forwards.append(copy)

    own = pltpu.make_async_copy(x_ref, g_ref.at[i, o, index[0]], own_sem)
    own.start()
    for s in range(streams):
        reached = [[0] for c in range(colours)]
        for step in range(bits):
            for at in range(max(len(r) for r in reached)):
                for c in range(colours):
                    mask = reached[c][at]
                    bit = 1 << (c + step) % bits
                    ensure(s, c, mask)
                    copy = pltpu.make_async_remote_copy(
                        src_ref=block(s, c, mask), dst_ref=g_ref.at[place(mask), o, index[s], c],
                        send_sem=send_sem.at[s, c, mask | bit], recv_sem=recv_sem.at[s, c, mask | bit],
                        device_id=to(base + place(bit), o), device_id_type=MESH,
                    )
                    copy.start()
                    copies[s, c, mask | bit] = copy
            for c in range(colours):
                bit = 1 << (c + step) % bits
                reached[c] = reached[c] + [mask | bit for mask in reached[c]]
    for s in range(streams):
        for mask in range(half):
            for c in range(colours):
                ensure(s, c, mask)
    own.wait()
    for copy in copies.values():
        copy.wait_send()
    for copy in exchange:
        copy.wait_send()
        if not first:
            copy.wait_recv()
    for copy in forwards:
        copy.wait()


def spread(x, y, half, ops, first):
    colours = x.shape[0]
    streams = 2 if first else 1
    shapes = [jax.ShapeDtypeStruct((half, ops, streams) + x.shape, x.dtype)]
    if not first:
        shapes.append(jax.ShapeDtypeStruct(y.shape, y.dtype))
    size = x.size * half * ops * streams * 2
    return pl.pallas_call(
        functools.partial(spread_kernel, half, ops, colours, first),
        out_shape=shapes,
        in_specs=[pl.BlockSpec(memory_space=pltpu.VMEM)] * 2,
        out_specs=[pl.BlockSpec(memory_space=pl.ANY)] * len(shapes),
        scratch_shapes=[
            pltpu.SemaphoreType.DMA,
            pltpu.SemaphoreType.DMA((colours,)),
            pltpu.SemaphoreType.DMA((colours,)),
            pltpu.SemaphoreType.DMA((streams, colours, half)),
            pltpu.SemaphoreType.DMA((streams, colours, half)),
            pltpu.SemaphoreType.DMA((streams, colours, half, ops)),
            pltpu.SemaphoreType.DMA((streams, colours, half, ops)),
        ],
        compiler_params=pltpu.CompilerParams(
            collective_id=1 if first else 2, has_side_effects=True
        ),
        cost_estimate=pl.CostEstimate(flops=0, bytes_accessed=16 * size, transcendentals=0),
        name="spread_first" if first else "spread_second",
    )(x, y)


def apply_kernel(
    channels, rows, roots, site_charges, load,
    order_ref, shift_ref, site_ref, psi_ref, left_ref, right_ref, out_ref, mixed
):
    @pl.loop(0, NQ)
    def _(g):
        for n in range(NPB):
            r = order_ref[g * NPB + n]
            terms = []
            for q in range(DP):
                h = lax.rem(2 * NQ - site_charges[q] - g, NQ)
                terms.append(
                    jnp.dot(left_ref[h], load(psi_ref, q * NB + r), preferred_element_type=jnp.float32)
                )
            for c in range(channels):
                for p in range(DP):
                    total = site_ref[(c * DP + p) * DP] * terms[0][c * rows:(c + 1) * rows]
                    for q in range(1, DP):
                        total += site_ref[(c * DP + p) * DP + q] * terms[q][c * rows:(c + 1) * rows]
                    total = total.astype(jnp.bfloat16)
                    for k in range(roots):
                        at = (p * roots + k) * rows
                        mixed[c, g, at:at + rows, n * B:(n + 1) * B] = total[:, k * B:(k + 1) * B]

    @pl.loop(0, NQ)
    def _(g):
        total = None
        for c in range(channels):
            source = lax.rem(g + shift_ref[c], NQ)
            term = lax.dot_general(
                mixed[c, source], right_ref[c, g], (((1,), (1,)), ((), ())),
                preferred_element_type=jnp.float32,
            )
            total = term if total is None else total + term
        for m in range(NPB):
            out_ref[order_ref[g * NPB + m]] = total[:, m * B:(m + 1) * B]


def apply_all(order, shift, site, psi, left, right, rows, roots, load):
    channels = right.shape[0]
    height = DP * roots * rows
    smem = pl.BlockSpec(memory_space=pltpu.SMEM)
    vmem = pl.BlockSpec(memory_space=pltpu.VMEM)
    return pl.pallas_call(
        functools.partial(apply_kernel, channels, rows, roots, site_charge_table, load),
        out_shape=jax.ShapeDtypeStruct((NB, height, B), jnp.float32),
        in_specs=[smem, smem, smem, vmem, vmem, vmem],
        out_specs=vmem,
        scratch_shapes=[pltpu.VMEM((channels, NQ, height, NPB * B), jnp.bfloat16)],
        compiler_params=pltpu.CompilerParams(vmem_limit_bytes=58 * 1024 * 1024),
        name="apply_all",
    )(order, shift, site, psi, left, right)


def timetable(bits, psi_orders, right_orders, psi_parts, left_parts, slot, delay, prepared):
    orders = {"psi": psi_orders, "right": right_orders}
    waiting, done = [], []
    landed = 0.0

    def open_node(family, s, c, mask, level, at):
        for n in range(level, bits):
            waiting.append((family, s, c, mask, n, at))

    for c in range(len(psi_orders[0])):
        open_node("psi", 0, c, 0, 0, 0.0)
    for c in range(len(right_orders[0])):
        open_node("right", 0, c, 0, 0, prepared)
    far = [("psi", c) for c in range(psi_parts)] + [("left", c) for c in range(left_parts)]
    far += [("right", c) for c in range(len(right_orders[0]))]
    free = [0.0] * bits
    far_free, now = 0.0, 0.0
    while waiting or far:
        for link in range(bits):
            if free[link] > now:
                continue
            if link == bits - 1 and far and far_free <= now:
                kind, c = far.pop(0)
                if kind != "right" or now >= prepared:
                    done.append((now, ("far", kind, c, 0)))
                    done.append((now + slot, ("far", kind, c, 1)))
                    free[link] = now + slot
                    far_free = now + 2 * slot
                    if kind != "left":
                        open_node(kind, 1, c, 0, 0, now + 2 * slot + 2 * delay)
                    continue
                far.insert(0, (kind, c))
            best = None
            for item in waiting:
                family, s, c, mask, n, at = item
                if orders[family][s][c][n] != link or at > now:
                    continue
                key = (family == "right", n - bits if n < bits - 1 else 0, n, at, s, c, mask)
                if best is None or key < best[0]:
                    best = (key, item)
            if best is None:
                continue
            family, s, c, mask, n, at = best[1]
            waiting.remove(best[1])
            done.append((now, ("hop", family, s, c, mask, n)))
            free[link] = now + slot
            arrival = now + slot + delay
            if family == "psi":
                landed = max(landed, arrival)
            open_node(family, s, c, mask | 1 << link, n + 1, arrival)
        now += slot / 16
    done.sort(key=lambda entry: entry[0])
    return done, landed, now + slot


def whole_kernel(
    half, ops, some, channels, site_charges,
    left_charge_ref, right_charge_ref, channel_ref, operator_ref,
    wave_ref, lt_ref, rt_ref, one_ref, two_ref,
    order_ref, rank_ref, left_order_ref, left_rank_ref, shift_ref, left_shift_ref, site_ref,
    psi, gathered, right, left, left_raw, mixed, part_sum, got_first, got_second, stage, away,
    swap, sorted_out, ready, landed,
    stage_sem, psend, precv, send_sem, recv_sem, fsend, frecv,
    rpsend, rprecv, rsend, rrecv, lsend, lrecv, lown, osend, orecv, osend2, orecv2,
    wsend, wrecv, asend, arecv, free_sem,
):
    bond = lax.axis_index("bond")
    o = lax.axis_index("op")
    bonds = 2 * half
    i = lax.rem(bond, half)
    part = bond // half
    base = bond - i
    partner = i + half * (1 - part)
    bits = half.bit_length() - 1
    rows = left.shape[1] // channels
    sub = rows // NPB
    fine = lt_ref.shape[3]
    streams = 2
    other = lax.rem(o + 1, ops)

    def place(mask):
        at = i
        for t in range(bits):
            if mask >> t & 1:
                at = at + (1 << t) * (1 - 2 * lax.rem(i // (1 << t), 2))
        return at

    def turn(x):
        return lax.rem(2 * x, half) + (2 * x) // half

    def to(bond_index, op_index):
        return {"bond": bond_index, "op": op_index}

    def remote(src, dst, send, recv, bond_index, op_index):
        return pltpu.make_async_remote_copy(
            src_ref=src, dst_ref=dst, send_sem=send, recv_sem=recv,
            device_id=to(bond_index, op_index), device_id_type=MESH,
        )

    barrier = pltpu.get_barrier_semaphore()
    for e in range(1, bonds):
        pl.semaphore_signal(
            barrier, inc=1, device_id=to(lax.rem(bond + e, bonds), o), device_id_type=MESH
        )
    pl.semaphore_signal(barrier, inc=1, device_id=to(bond, other), device_id_type=MESH)

    share = stage.shape[1]
    groups = stage.shape[2] // B
    load = pltpu.make_async_copy(wave_ref.at[:, pl.ds(o * share, share), :], stage, stage_sem)
    load.start()
    load.wait()
    tiles = share // sub
    for k in range(some):
        for at in range(groups):
            for t in range(tiles):
                psi[i, o, k, part, at * tiles + t] = stage[
                    part * some + k, t * sub:(t + 1) * sub, at * B:(at + 1) * B
                ].astype(jnp.bfloat16)
                away[k, at * tiles + t] = stage[
                    (1 - part) * some + k, t * sub:(t + 1) * sub, at * B:(at + 1) * B
                ].astype(jnp.bfloat16)
    pl.semaphore_wait(barrier, bonds)

    def spread(index, exchange, orders):
        colours = some
        copies, forwards, ready_set = {}, [], set()

        def slot(s, c, mask):
            return psi.at[place(mask), o, c, index[s]]

        def ensure(s, c, mask):
            if (s, c, mask) in ready_set:
                return
            ready_set.add((s, c, mask))
            if mask:
                copies[s, c, mask].wait_recv()
            elif s == 1 and exchange:
                exchange[c].wait_recv()
            copy = remote(slot(s, c, mask), slot(s, c, mask), fsend.at[s, c, mask],
                          frecv.at[s, c, mask], bond, other)
            copy.start()
            forwards.append(copy)

        def hop(s, c, mask, n):
            bit = 1 << orders[s][c][n]
            ensure(s, c, mask)
            copy = remote(slot(s, c, mask), slot(s, c, mask), send_sem.at[s, c, mask | bit],
                          recv_sem.at[s, c, mask | bit], base + place(bit), o)
            copy.start()
            copies[s, c, mask | bit] = copy

        def step(s, n):
            for at in range(1 << n):
                for c in range(colours):
                    hop(s, c, sum(1 << orders[s][c][b] for b in range(n) if at >> b & 1), n)

        def finish():
            for s in range(streams):
                for mask in range(half):
                    for c in range(colours):
                        ensure(s, c, mask)
            for copy in copies.values():
                copy.wait_send()
            for copy in exchange:
                copy.wait_send()
            for copy in forwards:
                copy.wait()

        return hop, step, finish

    exchange = []
    for c in range(some):
        exchange.append(remote(away.at[c], psi.at[i, o, c, part], psend.at[c], precv.at[c], partner, o))
    last = bits - 1
    turns = [(0, 1, last), (1, last, 0), (last, 0, 1)]
    psi_orders = [turns, [(0, last, 1), (1, last, 0), (last, 1, 0)]]
    right_orders = [[(last, 0, 1), (last, 1, 0), (0, last, 1), (1, last, 0)]] * 2
    paints = len(right_orders[0])
    wide = channels // paints
    psi_hop, unused, psi_finish = spread((part, 1 - part), exchange, psi_orders)
    plan, psi_landed, plan_end = timetable(
        bits, psi_orders, right_orders, some, paints, 2.8, 2.5, 6.0)
    plan = list(plan)

    def lead(until):
        while plan and plan[0][0] <= until:
            operation = plan.pop(0)[1]
            if operation[0] == "far":
                send_far(*operation[1:])
            elif operation[1] == "psi":
                psi_hop(*operation[2:])
            else:
                right_hop(*operation[2:])

    def send_far(kind, c, turn_of):
        if kind == "psi":
            item = [(None, exchange[c])]
        elif kind == "right":
            item = [(None, right_exchange[c])]
        else:
            item = left_copies[2 * c:2 * c + 2] + own_left[c:c + 1]
        ready_now = lax.rem(part + i // (half // 2), 2) == turn_of
        for when, copy in item:
            @pl.when(ready_now if when is None else when & ready_now)
            def _():
                copy.start()

    def tile(slot, c):
        return gathered.at[slot, pl.ds(c * wide, wide)]

    right_exchange = []
    for c in range(paints):
        right_exchange.append(remote(tile(bond, c), tile(bond, c), rpsend.at[c], rprecv.at[c], partner, o))
    right_copies, right_ready = {}, set()

    def right_ensure(s, c, mask):
        if (s, c, mask) in right_ready:
            return
        right_ready.add((s, c, mask))
        if mask:
            right_copies[s, c, mask].wait_recv()
        elif s == 1:
            right_exchange[c].wait_recv()

    def right_hop(s, c, mask, n):
        start = base if s == 0 else half - base
        bit = 1 << right_orders[s][c][n]
        right_ensure(s, c, mask)
        here = tile(start + place(mask), c)
        copy = remote(here, here, rsend.at[s, c, mask | bit], rrecv.at[s, c, mask | bit],
                      base + place(bit), o)
        copy.start()
        right_copies[s, c, mask | bit] = copy

    parity = lax.rem(bond, 2)

    def left_part(ref, c):
        return ref.at[pl.ds(c * wide, wide)]

    left_copies, own_left = [], []
    for c in range(paints):
        for h in range(2):
            target = h * half + turn(bond // 2)
            left_copies.append((target != bond, remote(
                left_part(lt_ref, c), left_part(left_raw.at[parity], c),
                lsend.at[h, c], lrecv.at[parity, c], target, o)))
        own_left.append((lax.rem(turn(bond // 2), half) == i, pltpu.make_async_copy(
            left_part(lt_ref, c), left_part(left_raw.at[parity], c), lown.at[c])))

    lead(2.0)
    for ref, order, rank in ((right_charge_ref, order_ref, rank_ref),
                             (left_charge_ref, left_order_ref, left_rank_ref)):
        @pl.loop(0, NB)
        def _(b):
            mine = ref[b]
            total = jnp.int32(0)
            for e in range(NB):
                ahead = (ref[e] < mine) | ((ref[e] == mine) & (e < b))
                total += jnp.where(ahead, 1, 0)
            rank[b] = total

        @pl.loop(0, NB)
        def _(b):
            total = jnp.int32(0)
            for e in range(NB):
                total += jnp.where(rank[e] == b, e, 0)
            order[b] = total

    @pl.loop(0, channels)
    def _(c):
        left_shift = channel_ref[o * channels + c, 0]
        move = channel_ref[o * channels + c, 1]
        left_shift_ref[c] = lax.rem(left_shift + NQ, NQ)
        shift_ref[c] = lax.rem(left_shift + move + 2 * NQ, NQ)
        for p in range(DP):
            for q in range(DP):
                gap = site_charges[p] - site_charges[q] - move + 4 * NQ
                site_ref[(c * DP + p) * DP + q] = jnp.where(
                    lax.rem(gap, NQ) == 0, operator_ref[c, p, q], 0.0)

    @pl.loop(0, channels)
    def _(c):
        for g in range(NQ):
            bands = []
            for m in range(NPB):
                r = order_ref[g * NPB + m]
                bands.append(jnp.concatenate(
                    [rt_ref[c, r, n].astype(jnp.float32) for n in range(NPB)], 1))
            gathered[bond, c, g] = jnp.concatenate(bands, 0).astype(jnp.bfloat16)

    lead(psi_landed)
    band = i // 2 + lax.rem(i, 2) * (half // 2)
    for t in range(2):
        source = 2 * band + t
        for c in range(paints):
            @pl.when(source != bond)
            def _():
                remote(left_part(lt_ref, c), left_part(left_raw.at[t], c), lsend.at[0, c],
                       lrecv.at[t, c], source, o).wait_recv()

            @pl.when(source == bond)
            def _():
                own_left[c][1].wait()

    @pl.loop(0, NQ)
    def _(h):
        for c in range(channels):
            slot = lax.rem(h + left_shift_ref[c], NQ)
            for m in range(NPB):
                r = left_order_ref[slot * NPB + m]
                pieces = []
                for t in range(2):
                    pieces.append(jnp.concatenate(
                        [left_raw[t, c, r, n].astype(jnp.float32) for n in range(NPB)], 1))
                at = c * rows + m * sub
                left[h, at:at + sub] = jnp.concatenate(pieces, 0).astype(jnp.bfloat16)

    psi_finish()

    def left_dots(fetch, first, count):
        @pl.loop(first, first + count)
        def _(g):
            for n in range(NPB):
                terms = []
                for q in range(DP):
                    h = lax.rem(2 * NQ - site_charges[q] - g, NQ)
                    terms.append(
                        jnp.dot(left[h], fetch(q, g, n), preferred_element_type=jnp.float32)
                    )
                for c in range(channels):
                    for p in range(DP):
                        total = site_ref[(c * DP + p) * DP] * terms[0][c * rows:(c + 1) * rows]
                        for q in range(1, DP):
                            total += site_ref[(c * DP + p) * DP + q] * terms[q][c * rows:(c + 1) * rows]
                        total = total.astype(jnp.bfloat16)
                        for k in range(some):
                            at = (p * some + k) * rows
                            mixed[c, g, at:at + rows, n * B:(n + 1) * B] = total[:, k * B:(k + 1) * B]

    def fetch_first(q, g, n):
        r = order_ref[g * NPB + n]
        owner = q * (NB // groups) + r // groups
        at = lax.rem(r, groups)
        t, j = owner // half, lax.rem(owner, half)
        return jnp.concatenate([
            jnp.concatenate([
                psi[j, e, k, t, pl.ds(at * tiles, tiles)].reshape(share, B) for e in range(ops)
            ], 0) for k in range(some)
        ], 1)

    slices = NQ // 2
    for g in range(slices):
        left_dots(fetch_first, g * NQ // slices, NQ // slices)
        lead(psi_landed + (g + 1) * (plan_end - psi_landed) / slices)
    lead(plan_end)
    for t in range(bits):
        pl.semaphore_signal(free_sem, inc=1, device_id=to(base + place(1 << t), o), device_id_type=MESH)
    pl.semaphore_signal(free_sem, inc=1, device_id=to(bond, other), device_id_type=MESH)

    for s in range(streams):
        for c in range(paints):
            for mask in range(half):
                right_ensure(s, c, mask)
    for copy in right_exchange:
        copy.wait_send()
    for copy in right_copies.values():
        copy.wait_send()
    for away_from_here, copy in left_copies:
        @pl.when(away_from_here)
        def _():
            copy.wait_send()

    def right_dots(g):
        total = None
        for c in range(channels):
            source = lax.rem(g + shift_ref[c], NQ)
            term = lax.dot_general(
                mixed[c, source], right[c, g], (((1,), (1,)), ((), ())),
                preferred_element_type=jnp.float32,
            )
            total = term if total is None else total + term
        return total

    own_half = DP // ops * some * rows

    @pl.loop(0, NQ)
    def _(g):
        for c in range(channels):
            for u in range(bonds // 2):
                pair = [gathered[2 * u + t, c, g].astype(jnp.float32) for t in range(2)]
                for m in range(NPB):
                    at = m * B + u * sub
                    right[c, g, at:at + sub] = jnp.concatenate(
                        [x[m * fine:(m + 1) * fine] for x in pair], 0).astype(jnp.bfloat16)
        total = right_dots(g)
        for e in range(ops):
            part_sum[g, e] = total[e * own_half:(e + 1) * own_half]
        remote(part_sum.at[g, other], got_first.at[g], osend.at[g], orecv.at[g], bond, other).start()

    pl.semaphore_wait(free_sem, bits + 1)

    @pl.loop(0, NQ)
    def _(g):
        remote(part_sum.at[g, other], got_first.at[g], osend.at[g], orecv.at[g], bond, other).wait()
        total = (part_sum[g, o] + got_first[g]).astype(jnp.bfloat16)
        for p in range(DP // ops):
            for k in range(some):
                for m in range(NPB):
                    at = ((p * some + k) * NPB + m) * sub
                    for n in range(NPB):
                        psi[i, o, k, p, m * NB + g * NPB + n] = total[at:at + sub, n * B:(n + 1) * B]

    unused, again_step, again_finish = spread((0, 1), [], [turns, turns])
    again_step(0, 0)
    again_step(1, 0)
    for n in range(1, bits):
        again_step(0, n)
        again_step(1, n)
    again_finish()

    holder = turn(i)
    wanted = psi.at[holder, o, :, :, pl.ds((1 - part) * NB, NB)]
    trade = remote(wanted, swap, wsend, wrecv, partner, o)
    trade.start()

    def slot_of(x):
        return lax.rem(2 * x, half) + (2 * x) // half if not isinstance(x, int) else (2 * x) % half + (2 * x) // half

    def fetch_second(q, g, n):
        per = DP // ops
        return jnp.concatenate([
            jnp.concatenate([
                psi[slot_of(x), q // per, k, q % per, m * NB + g * NPB + n]
                for m in range(NPB) for x in range(half)
            ], 0) for k in range(some)
        ], 1)

    left_dots(fetch_second, 0, NQ)

    @pl.loop(0, NQ)
    def _(g):
        total = right_dots(g)
        for x in range(DP * some):
            for m in range(NPB):
                at = x * rows + m * sub
                part_sum[g, m, x * sub:(x + 1) * sub] = total[at:at + sub]
        remote(part_sum.at[g, other], got_second.at[g], osend2.at[g], orecv2.at[g], bond, other).start()

    @pl.loop(0, NQ)
    def _(g):
        remote(part_sum.at[g, other], got_second.at[g], osend2.at[g], orecv2.at[g], bond, other).wait()
        total = (part_sum[g, o] + got_second[g]).astype(jnp.bfloat16)
        for n in range(NPB):
            for x in range(DP * some):
                sorted_out[g * NPB + n, x] = total[x * sub:(x + 1) * sub, n * B:(n + 1) * B]

    for r in range(NB):
        s = rank_ref[r]
        for p in range(DP):
            for k in range(some):
                ready[p * (NB // groups) + r // groups, k, r % groups] = sorted_out[s, p * some + k]

    sends = []
    for e in range(1, bonds):
        target = lax.rem(bond + e, bonds)
        copy = remote(ready.at[target], landed.at[bond], asend.at[e], arecv.at[e], target, o)
        copy.start()
        sends.append(copy)

    trade.wait()
    for p in range(DP // ops):
        for r in range(NB):
            s = rank_ref[r]
            for k in range(some):
                cols = slice((p * NB + r) * B, (p * NB + r + 1) * B)
                one_ref[part * some + k, :, cols] = psi[
                    holder, o, k, p, part * NB + s].astype(jnp.float32)
                one_ref[(1 - part) * some + k, :, cols] = swap[k, p, s].astype(jnp.float32)

    landed[bond] = ready[bond]
    for copy in sends:
        copy.wait()
    for s in range(bonds):
        x = s % half
        spot = x // 2 + (x % 2) * (half // 2)
        for k in range(some):
            for at in range(groups):
                two_ref[(s // half) * some + k, spot * sub:(spot + 1) * sub, at * B:(at + 1) * B] = (
                    landed[s, k, at].astype(jnp.float32))


def whole(wave, left_tiles, right_tiles, tables, bonds, ops):
    roots, sector_rows, strip = wave.shape
    channels = left_tiles.shape[0]
    half = bonds // 2
    bits = half.bit_length() - 1
    some = roots // 2
    fine = left_tiles.shape[3]
    sub = 2 * fine
    rows = NPB * sub
    share = sector_rows // ops
    groups = strip // B
    height = DP * some * rows
    paints = 4
    vmem = pl.BlockSpec(memory_space=pltpu.VMEM)
    smem = pl.BlockSpec(memory_space=pltpu.SMEM)
    dma = pltpu.SemaphoreType.DMA
    bf, f32 = jnp.bfloat16, jnp.float32
    return pl.pallas_call(
        functools.partial(whole_kernel, half, ops, some, channels, site_charge_table),
        out_shape=[
            jax.ShapeDtypeStruct((roots, NPB * B // bonds, DP // ops * NB * B), f32),
            jax.ShapeDtypeStruct((roots, share, strip), f32),
        ],
        in_specs=[smem] * 4 + [pl.BlockSpec(memory_space=pl.ANY), vmem, vmem],
        out_specs=[vmem, vmem],
        scratch_shapes=[pltpu.SMEM((NB,), jnp.int32)] * 4 + [pltpu.SMEM((channels,), jnp.int32)] * 2 + [
            pltpu.SMEM((channels * DP * DP,), f32),
            pltpu.VMEM((half, ops, some, 2, groups * share // sub, sub, B), bf),
            pltpu.VMEM((bonds, channels, NQ, NPB * fine, NPB * B), bf),
            pltpu.VMEM((channels, NQ, NPB * B, NPB * B), bf),
            pltpu.VMEM((NQ, channels * rows, NPB * B), bf),
            pltpu.VMEM((2,) + left_tiles.shape, bf),
            pltpu.VMEM((channels, NQ, height, NPB * B), bf),
            pltpu.VMEM((NQ, ops, height // ops, NPB * B), f32),
            pltpu.VMEM((NQ, height // ops, NPB * B), f32),
            pltpu.VMEM((NQ, height // ops, NPB * B), f32),
            pltpu.VMEM((roots, share, strip), f32),
            pltpu.VMEM((some, groups * share // sub, sub, B), bf),
            pltpu.VMEM((some, DP // ops, NB, sub, B), bf),
            pltpu.VMEM((NB, DP * some, sub, B), bf),
            pltpu.VMEM((bonds, some, groups, sub, B), bf),
            pltpu.VMEM((bonds, some, groups, sub, B), bf),
            dma, dma((some,)), dma((some,)),
            dma((2, some, half)), dma((2, some, half)), dma((2, some, half)), dma((2, some, half)),
            dma((paints,)), dma((paints,)), dma((2, paints, half)), dma((2, paints, half)),
            dma((2, paints)), dma((2, paints)), dma((paints,)),
            dma((NQ,)), dma((NQ,)), dma((NQ,)), dma((NQ,)),
            dma, dma, dma((bonds,)), dma((bonds,)),
            pltpu.SemaphoreType.REGULAR,
        ],
        compiler_params=pltpu.CompilerParams(
            collective_id=3, has_side_effects=True, vmem_limit_bytes=67043328
        ),
        name="whole",
    )(*tables, wave, left_tiles, right_tiles)


def local_whole(
    wavefunction, left_tiles, right_tiles, site_operators, left_charge, right_charge, channel_charge
):
    tables = (left_charge, right_charge, channel_charge, site_operators)
    return tuple(whole(
        wavefunction, left_tiles, right_tiles, tables, lax.axis_size("bond"), lax.axis_size("op")
    ))


def fits(mesh, wavefunction, left_tiles):
    bonds, ops = mesh.shape["bond"], mesh.shape["op"]
    strip = wavefunction.shape[2] // bonds
    fine = left_tiles.shape[3] // bonds
    channels = left_tiles.shape[0] // ops
    return (
        ops == NPB and bonds == NB and strip % B == 0 and 2 * fine * (bonds // 2) == B
        and channels % 4 == 0 and NPB * fine == 16
    )


def local(
    wavefunction, left_tiles, right_tiles, site_operators, left_charge, right_charge, channel_charge
):
    bonds = lax.axis_size("bond")
    ops = lax.axis_size("op")
    bond = lax.axis_index("bond")
    op = lax.axis_index("op")
    roots, sector_rows, strip = wavefunction.shape
    channels = site_operators.shape[0]
    half = bonds // 2
    part = bond // half
    some = roots // 2
    chunk = left_tiles.shape[3]
    band = 2 * chunk
    rows = NPB * band
    held = -(-rows // 16) * 16
    width = min(strip, B)
    groups = strip // width
    own_charge = lax.dynamic_slice_in_dim(channel_charge, op * channels, channels, 0)
    left_order = jnp.argsort(left_charge, stable=True).astype(jnp.int32)
    right_order = jnp.argsort(right_charge, stable=True).astype(jnp.int32)
    shift = (own_charge[:, 0] + own_charge[:, 1]) % NQ
    site = site_masks(site_operators, own_charge).reshape(-1)

    right = right_tiles[:, right_order].transpose(0, 1, 3, 2, 4).reshape(
        channels, NB, chunk, NPB * B
    )
    right = lax.all_gather(right, "bond", axis=2, tiled=True).reshape(
        channels, NQ, NPB * B, NPB * B
    )

    even = [(b, b // 2 + (b % 2) * half) for b in range(bonds)]
    odd = [(b, b // 2 + (1 - b % 2) * half) for b in range(bonds)]
    one = lax.ppermute(left_tiles, "bond", even)
    two = lax.ppermute(left_tiles, "bond", odd)
    low = jnp.where(part == 0, one, two)
    high = jnp.where(part == 0, two, one)
    left = jnp.concatenate([low, high], axis=3)
    left_slots = ((jnp.arange(NQ)[:, None] + own_charge[None, :, 0]) % NQ)[:, :, None] * NPB + jnp.arange(NPB)
    left = left[jnp.arange(channels)[None, :, None], left_order[left_slots]]
    left = left.transpose(0, 1, 2, 4, 3, 5).reshape(NQ, channels, rows, NPB * B)
    left = jnp.pad(left, ((0, 0), (0, 0), (0, held - rows), (0, 0)))
    left = left.reshape(NQ, channels * held, NPB * B)

    share = sector_rows // ops
    psi = lax.dynamic_slice_in_dim(wavefunction, op * share, share, 1).astype(jnp.bfloat16)
    psi = psi.reshape(2, some, share, groups, width).transpose(0, 1, 3, 2, 4)
    kept = lax.dynamic_index_in_dim(psi, part, 0, keepdims=False)
    other = lax.dynamic_index_in_dim(psi, 1 - part, 0, keepdims=False)
    (psi,) = spread(kept, other, half, ops, True)

    def load_whole(ref, block):
        return ref[block]

    def load_first(ref, block):
        owner = block // groups
        t, j, at = owner // half, lax.rem(owner, half), lax.rem(block, groups)
        return jnp.concatenate(
            [jnp.concatenate([ref[j, o, t, k, at] for o in range(ops)], 0) for k in range(some)], 1
        )

    load = load_first
    if width < B:
        psi = psi.reshape(half, ops, 2, some, share, strip).transpose(2, 0, 5, 1, 4, 3)
        psi = psi.reshape(DP * NB, B, sector_rows, some).transpose(0, 2, 3, 1)
        psi = psi.reshape(DP * NB, sector_rows, some * B)
        load = load_whole
    elif share % 16:
        psi = psi.transpose(2, 0, 4, 1, 5, 3, 6).reshape(DP * NB, sector_rows, some * B)
        load = load_whole

    def unpack(result):
        result = result.reshape(NB, DP, some, held, B)[:, :, :, :rows]
        return result.reshape(NB, DP, some, NPB, band, B)

    def summed_share(parts, axis):
        size = parts.shape[axis] // ops
        total = lax.dynamic_slice_in_dim(parts, op * size, size, axis)
        for e in range(1, ops):
            to = (op + e) % ops
            sent = lax.dynamic_slice_in_dim(parts, to * size, size, axis)
            total += lax.ppermute(sent, "op", [(o, (o + e) % ops) for o in range(ops)])
        return total

    first = unpack(apply_all(right_order, shift, site, psi, left, right, held, some, load))
    turned = (DP * NB, some, NPB, band, B)
    if DP % ops == 0:
        first = summed_share(first, 1).transpose(1, 0, 2, 3, 4, 5)
        first = first.reshape((DP * NB // ops,) + turned[1:])
    else:
        first = summed_share(first.transpose(1, 0, 2, 3, 4, 5).reshape(turned), 0)
    blocks = first.shape[0]

    mine = lax.dynamic_index_in_dim(first, part, 2, keepdims=False)
    theirs = lax.dynamic_index_in_dim(first, 1 - part, 2, keepdims=False)
    again = first.astype(jnp.bfloat16).transpose(1, 0, 2, 3, 4)
    again, back = spread(again, theirs.astype(jnp.bfloat16), half, ops, False)
    back = back.astype(jnp.float32)
    both = jnp.stack([jnp.where(part == 0, mine, back), jnp.where(part == 0, back, mine)])
    sigma_one = both.transpose(0, 2, 3, 1, 4).reshape(roots, band, blocks * B)

    def load_second(ref, block):
        o, at = block // blocks, lax.rem(block, blocks)
        return jnp.concatenate(
            [
                jnp.concatenate([ref[j, o, 0, k, at, m] for m in range(NPB) for j in range(half)], 0)
                for k in range(some)
            ], 1,
        )

    load = load_second
    if band % 16:
        again = again[:, :, 0].transpose(1, 3, 4, 0, 5, 2, 6)
        again = again.reshape(DP * NB, sector_rows, some * B)
        load = load_whole
    second = unpack(apply_all(right_order, shift, site, again, left, right, held, some, load))
    if ops == NPB:
        second = summed_share(second, 3)
    else:
        second = lax.psum(second, "op")
    tiles = second.shape[3]
    second = second.astype(jnp.bfloat16).transpose(2, 3, 4, 1, 0, 5)
    second = second.reshape(some, tiles * band, bonds, strip).transpose(2, 0, 1, 3)
    second = lax.all_to_all(second, "bond", split_axis=0, concat_axis=0, tiled=True)
    second = second.reshape(2, half, some, tiles, band, strip).transpose(0, 2, 3, 1, 4, 5)
    second = second.reshape(roots, tiles * B, strip).astype(jnp.float32)
    if ops != NPB:
        second = lax.dynamic_slice_in_dim(second, op * share, share, 1)
    return (sigma_one, second)


def solution(mesh):
    def run(*args):
        body = local_whole if fits(mesh, args[0], args[1]) else local
        return jax.shard_map(
            body,
            mesh=mesh,
            in_specs=(
                P(None, None, "bond"),
                P("op", None, None, "bond", None),
                P("op", None, None, "bond", None),
                P("op", None, None),
                P(),
                P(),
                P(),
            ),
            out_specs=(P(None, "bond", "op"), P(None, "op", "bond")),
            check_vma=False,
        )(*args)

    return run
```

```python
import functools

import jax
import jax.numpy as jnp
from jax import lax
from jax.experimental import pallas as pl
from jax.experimental.pallas import tpu as pltpu
from jax.sharding import PartitionSpec as P

M = 2048
B = 128
NQ = 8
DP = 4
NB = 16
NPB = 2

site_charge_table = (0, 1, 1, 2)
MESH = pl.DeviceIdType.MESH


def site_masks(site_operators, channel_charge):
    site_charge = jnp.array(site_charge_table, dtype=jnp.int32)
    charge_step = site_charge[:, None] - site_charge[None, :]
    allowed = (charge_step[None, :, :] - channel_charge[:, 1][:, None, None]) % NQ == 0
    return jnp.where(allowed, site_operators, jnp.zeros_like(site_operators))


def spread_kernel(half, ops, colours, first, *refs):
    if first:
        x_ref, y_ref, g_ref = refs[:3]
        z_ref = None
        scratch = refs[3:]
    else:
        x_ref, y_ref, g_ref, z_ref = refs[:4]
        scratch = refs[4:]
    own_sem, psend, precv, send_sem, recv_sem, fsend, frecv = scratch
    bond = lax.axis_index("bond")
    o = lax.axis_index("op")
    i = lax.rem(bond, half)
    part = bond // half
    base = bond - i
    partner = i + half * (1 - part)
    bits = half.bit_length() - 1
    streams = 2 if first else 1

    def place(mask):
        at = i
        for t in range(bits):
            if mask >> t & 1:
                at = at + (1 << t) * (1 - 2 * lax.rem(i // (1 << t), 2))
        return at

    def to(bond_index, op_index):
        return {"bond": bond_index, "op": op_index}

    barrier = pltpu.get_barrier_semaphore()
    for t in range(bits):
        pl.semaphore_signal(
            barrier, inc=1, device_id=to(base + place(1 << t), o), device_id_type=MESH
        )
    pl.semaphore_signal(barrier, inc=1, device_id=to(partner, o), device_id_type=MESH)
    for e in range(1, ops):
        pl.semaphore_signal(
            barrier, inc=1, device_id=to(bond, lax.rem(o + e, ops)), device_id_type=MESH
        )
    pl.semaphore_wait(barrier, bits + ops)

    index = (part, 1 - part) if first else (0,)
    exchange = []
    for c in range(colours if first else 1):
        exchange.append(pltpu.make_async_remote_copy(
            src_ref=y_ref.at[c] if first else y_ref,
            dst_ref=g_ref.at[i, o, part, c] if first else z_ref,
            send_sem=psend.at[c], recv_sem=precv.at[c],
            device_id=to(partner, o), device_id_type=MESH,
        ))
        exchange[-1].start()

    copies = {}
    forwards = []
    ready = set()

    def block(s, c, mask):
        if s == 0 and mask == 0:
            return x_ref.at[c]
        return g_ref.at[place(mask), o, index[s], c]

    def ensure(s, c, mask):
        if (s, c, mask) in ready:
            return
        ready.add((s, c, mask))
        if mask:
            copies[s, c, mask].wait_recv()
        elif s == 1:
            exchange[c].wait_recv()
        for e in range(1, ops):
            copy = pltpu.make_async_remote_copy(
                src_ref=block(s, c, mask), dst_ref=g_ref.at[place(mask), o, index[s], c],
                send_sem=fsend.at[s, c, mask, e], recv_sem=frecv.at[s, c, mask, e],
                device_id=to(bond, lax.rem(o + e, ops)), device_id_type=MESH,
            )
            copy.start()
            forwards.append(copy)

    own = pltpu.make_async_copy(x_ref, g_ref.at[i, o, index[0]], own_sem)
    own.start()
    for s in range(streams):
        reached = [[0] for c in range(colours)]
        for step in range(bits):
            for at in range(max(len(r) for r in reached)):
                for c in range(colours):
                    mask = reached[c][at]
                    bit = 1 << (c + step) % bits
                    ensure(s, c, mask)
                    copy = pltpu.make_async_remote_copy(
                        src_ref=block(s, c, mask), dst_ref=g_ref.at[place(mask), o, index[s], c],
                        send_sem=send_sem.at[s, c, mask | bit], recv_sem=recv_sem.at[s, c, mask | bit],
                        device_id=to(base + place(bit), o), device_id_type=MESH,
                    )
                    copy.start()
                    copies[s, c, mask | bit] = copy
            for c in range(colours):
                bit = 1 << (c + step) % bits
                reached[c] = reached[c] + [mask | bit for mask in reached[c]]
    for s in range(streams):
        for mask in range(half):
            for c in range(colours):
                ensure(s, c, mask)
    own.wait()
    for copy in copies.values():
        copy.wait_send()
    for copy in exchange:
        copy.wait_send()
        if not first:
            copy.wait_recv()
    for copy in forwards:
        copy.wait()


def spread(x, y, half, ops, first):
    colours = x.shape[0]
    streams = 2 if first else 1
    shapes = [jax.ShapeDtypeStruct((half, ops, streams) + x.shape, x.dtype)]
    if not first:
        shapes.append(jax.ShapeDtypeStruct(y.shape, y.dtype))
    size = x.size * half * ops * streams * 2
    return pl.pallas_call(
        functools.partial(spread_kernel, half, ops, colours, first),
        out_shape=shapes,
        in_specs=[pl.BlockSpec(memory_space=pltpu.VMEM)] * 2,
        out_specs=[pl.BlockSpec(memory_space=pl.ANY)] * len(shapes),
        scratch_shapes=[
            pltpu.SemaphoreType.DMA,
            pltpu.SemaphoreType.DMA((colours,)),
            pltpu.SemaphoreType.DMA((colours,)),
            pltpu.SemaphoreType.DMA((streams, colours, half)),
            pltpu.SemaphoreType.DMA((streams, colours, half)),
            pltpu.SemaphoreType.DMA((streams, colours, half, ops)),
            pltpu.SemaphoreType.DMA((streams, colours, half, ops)),
        ],
        compiler_params=pltpu.CompilerParams(
            collective_id=1 if first else 2, has_side_effects=True
        ),
        cost_estimate=pl.CostEstimate(flops=0, bytes_accessed=16 * size, transcendentals=0),
        name="spread_first" if first else "spread_second",
    )(x, y)


def apply_kernel(
    channels, rows, roots, site_charges, load,
    order_ref, shift_ref, site_ref, psi_ref, left_ref, right_ref, out_ref, mixed
):
    @pl.loop(0, NQ)
    def _(g):
        for n in range(NPB):
            r = order_ref[g * NPB + n]
            terms = []
            for q in range(DP):
                h = lax.rem(2 * NQ - site_charges[q] - g, NQ)
                terms.append(
                    jnp.dot(left_ref[h], load(psi_ref, q * NB + r), preferred_element_type=jnp.float32)
                )
            for c in range(channels):
                for p in range(DP):
                    total = site_ref[(c * DP + p) * DP] * terms[0][c * rows:(c + 1) * rows]
                    for q in range(1, DP):
                        total += site_ref[(c * DP + p) * DP + q] * terms[q][c * rows:(c + 1) * rows]
                    total = total.astype(jnp.bfloat16)
                    for k in range(roots):
                        at = (p * roots + k) * rows
                        mixed[c, g, at:at + rows, n * B:(n + 1) * B] = total[:, k * B:(k + 1) * B]

    @pl.loop(0, NQ)
    def _(g):
        total = None
        for c in range(channels):
            source = lax.rem(g + shift_ref[c], NQ)
            term = lax.dot_general(
                mixed[c, source], right_ref[c, g], (((1,), (1,)), ((), ())),
                preferred_element_type=jnp.float32,
            )
            total = term if total is None else total + term
        for m in range(NPB):
            out_ref[order_ref[g * NPB + m]] = total[:, m * B:(m + 1) * B]


def apply_all(order, shift, site, psi, left, right, rows, roots, load):
    channels = right.shape[0]
    height = DP * roots * rows
    smem = pl.BlockSpec(memory_space=pltpu.SMEM)
    vmem = pl.BlockSpec(memory_space=pltpu.VMEM)
    return pl.pallas_call(
        functools.partial(apply_kernel, channels, rows, roots, site_charge_table, load),
        out_shape=jax.ShapeDtypeStruct((NB, height, B), jnp.float32),
        in_specs=[smem, smem, smem, vmem, vmem, vmem],
        out_specs=vmem,
        scratch_shapes=[pltpu.VMEM((channels, NQ, height, NPB * B), jnp.bfloat16)],
        compiler_params=pltpu.CompilerParams(vmem_limit_bytes=58 * 1024 * 1024),
        name="apply_all",
    )(order, shift, site, psi, left, right)


def timetable(bits, psi_orders, right_orders, psi_parts, left_parts, slot, delay, prepared):
    orders = {"psi": psi_orders, "right": right_orders}
    waiting, done = [], []
    landed = 0.0

    def open_node(family, s, c, mask, level, at):
        for n in range(level, bits):
            waiting.append((family, s, c, mask, n, at))

    for c in range(len(psi_orders[0])):
        open_node("psi", 0, c, 0, 0, 0.0)
    for c in range(len(right_orders[0])):
        open_node("right", 0, c, 0, 0, prepared)
    far = [("psi", c) for c in range(psi_parts)] + [("left", c) for c in range(left_parts)]
    far += [("right", c) for c in range(len(right_orders[0]))]
    free = [0.0] * bits
    far_free, now = 0.0, 0.0
    while waiting or far:
        for link in range(bits):
            if free[link] > now:
                continue
            if link == bits - 1 and far and far_free <= now:
                kind, c = far.pop(0)
                if kind != "right" or now >= prepared:
                    done.append((now, ("far", kind, c, 0)))
                    done.append((now + slot, ("far", kind, c, 1)))
                    free[link] = now + slot
                    far_free = now + 2 * slot
                    if kind != "left":
                        open_node(kind, 1, c, 0, 0, now + 2 * slot + 2 * delay)
                    continue
                far.insert(0, (kind, c))
            best = None
            for item in waiting:
                family, s, c, mask, n, at = item
                if orders[family][s][c][n] != link or at > now:
                    continue
                key = (family == "right", n - bits if n < bits - 1 else 0, n, at, s, c, mask)
                if best is None or key < best[0]:
                    best = (key, item)
            if best is None:
                continue
            family, s, c, mask, n, at = best[1]
            waiting.remove(best[1])
            done.append((now, ("hop", family, s, c, mask, n)))
            free[link] = now + slot
            arrival = now + slot + delay
            if family == "psi":
                landed = max(landed, arrival)
            open_node(family, s, c, mask | 1 << link, n + 1, arrival)
        now += slot / 16
    done.sort(key=lambda entry: entry[0])
    return done, landed, now + slot


def whole_kernel(
    half, ops, some, channels, site_charges,
    left_charge_ref, right_charge_ref, channel_ref, operator_ref,
    wave_ref, lt_ref, rt_ref, one_ref, two_ref,
    order_ref, rank_ref, left_order_ref, left_rank_ref, shift_ref, left_shift_ref, site_ref, pick_ref, products,
    psi, gathered, right, left, left_raw, mixed, part_sum, got_first, got_second, stage, away,
    swap, sorted_out, ready, landed,
    stage_sem, psend, precv, send_sem, recv_sem, fsend, frecv,
    rpsend, rprecv, rsend, rrecv, lsend, lrecv, lown, osend, orecv, osend2, orecv2,
    wsend, wrecv, asend, arecv, free_sem,
):
    bond = lax.axis_index("bond")
    o = lax.axis_index("op")
    bonds = 2 * half
    i = lax.rem(bond, half)
    part = bond // half
    base = bond - i
    partner = i + half * (1 - part)
    bits = half.bit_length() - 1
    rows = left.shape[1] // channels
    sub = rows // NPB
    fine = lt_ref.shape[3]
    streams = 2
    most = max(site_charges.count(x) for x in site_charges)
    other = lax.rem(o + 1, ops)

    def place(mask):
        at = i
        for t in range(bits):
            if mask >> t & 1:
                at = at + (1 << t) * (1 - 2 * lax.rem(i // (1 << t), 2))
        return at

    def turn(x):
        return lax.rem(2 * x, half) + (2 * x) // half

    def to(bond_index, op_index):
        return {"bond": bond_index, "op": op_index}

    def remote(src, dst, send, recv, bond_index, op_index):
        return pltpu.make_async_remote_copy(
            src_ref=src, dst_ref=dst, send_sem=send, recv_sem=recv,
            device_id=to(bond_index, op_index), device_id_type=MESH,
        )

    barrier = pltpu.get_barrier_semaphore()
    for e in range(1, bonds):
        pl.semaphore_signal(
            barrier, inc=1, device_id=to(lax.rem(bond + e, bonds), o), device_id_type=MESH
        )
    pl.semaphore_signal(barrier, inc=1, device_id=to(bond, other), device_id_type=MESH)

    share = stage.shape[1]
    groups = stage.shape[2] // B
    load = pltpu.make_async_copy(wave_ref.at[:, pl.ds(o * share, share), :], stage, stage_sem)
    load.start()
    load.wait()
    tiles = share // sub
    for k in range(some):
        for at in range(groups):
            for t in range(tiles):
                psi[i, o, k, part, at * tiles + t] = stage[
                    part * some + k, t * sub:(t + 1) * sub, at * B:(at + 1) * B
                ].astype(jnp.bfloat16)
                away[k, at * tiles + t] = stage[
                    (1 - part) * some + k, t * sub:(t + 1) * sub, at * B:(at + 1) * B
                ].astype(jnp.bfloat16)
    pl.semaphore_wait(barrier, bonds)

    def spread(view, exchange, orders):
        colours = some
        copies, forwards, ready_set = {}, [[], []], set()

        def slot(s, c, mask):
            return view(place(mask), c, s)

        def ensure(s, c, mask):
            if (s, c, mask) in ready_set:
                return
            ready_set.add((s, c, mask))
            if mask:
                copies[s, c, mask].wait_recv()
            elif s == 1 and exchange:
                exchange[c].wait_recv()
            copy = remote(slot(s, c, mask), slot(s, c, mask), fsend.at[s, c, mask],
                          frecv.at[s, c, mask], bond, other)
            copy.start()
            forwards[s].append(copy)

        def hop(s, c, mask, n):
            bit = 1 << orders[s][c][n]
            ensure(s, c, mask)
            copy = remote(slot(s, c, mask), slot(s, c, mask), send_sem.at[s, c, mask | bit],
                          recv_sem.at[s, c, mask | bit], base + place(bit), o)
            copy.start()
            copies[s, c, mask | bit] = copy

        def step(s, n):
            for at in range(1 << n):
                for c in range(colours):
                    hop(s, c, sum(1 << orders[s][c][b] for b in range(n) if at >> b & 1), n)

        def arrive(s):
            for mask in range(half):
                for c in range(colours):
                    ensure(s, c, mask)
            while forwards[s]:
                forwards[s].pop().wait()

        def finish():
            for s in range(streams):
                arrive(s)
            for copy in copies.values():
                copy.wait_send()
            for copy in exchange:
                copy.wait_send()

        return hop, step, arrive, finish

    exchange = []
    for c in range(some):
        exchange.append(remote(away.at[c], psi.at[i, o, c, part], psend.at[c], precv.at[c], partner, o))
    last = bits - 1
    turns = [(0, 1, last), (1, last, 0), (last, 0, 1)]
    psi_orders = [turns, [(0, last, 1), (1, last, 0), (last, 1, 0)]]
    right_orders = [[(last, 0, 1), (last, 1, 0), (0, last, 1), (1, last, 0)]] * 2
    paints = len(right_orders[0])
    wide = channels // paints
    def view_first(j, c, s):
        return psi.at[j, o, c, part if s == 0 else 1 - part]

    psi_hop, unused, unused, psi_finish = spread(view_first, exchange, psi_orders)
    plan, psi_landed, plan_end = timetable(
        bits, psi_orders, right_orders, some, paints, 2.8, 2.5, 6.0)
    plan = list(plan)

    def lead(until):
        while plan and plan[0][0] <= until:
            operation = plan.pop(0)[1]
            if operation[0] == "far":
                send_far(*operation[1:])
            elif operation[1] == "psi":
                psi_hop(*operation[2:])
            else:
                right_hop(*operation[2:])

    def send_far(kind, c, turn_of):
        if kind == "psi":
            item = [(None, exchange[c])]
        elif kind == "right":
            item = [(None, right_exchange[c])]
        else:
            item = left_copies[2 * c:2 * c + 2] + own_left[c:c + 1]
        ready_now = lax.rem(part + i // (half // 2), 2) == turn_of
        for when, copy in item:
            @pl.when(ready_now if when is None else when & ready_now)
            def _():
                copy.start()

    def tile(slot, c):
        return gathered.at[slot, pl.ds(c * wide, wide)]

    right_exchange = []
    for c in range(paints):
        right_exchange.append(remote(tile(bond, c), tile(bond, c), rpsend.at[c], rprecv.at[c], partner, o))
    right_copies, right_ready = {}, set()

    def right_ensure(s, c, mask):
        if (s, c, mask) in right_ready:
            return
        right_ready.add((s, c, mask))
        if mask:
            right_copies[s, c, mask].wait_recv()
        elif s == 1:
            right_exchange[c].wait_recv()

    def right_hop(s, c, mask, n):
        start = base if s == 0 else half - base
        bit = 1 << right_orders[s][c][n]
        right_ensure(s, c, mask)
        here = tile(start + place(mask), c)
        copy = remote(here, here, rsend.at[s, c, mask | bit], rrecv.at[s, c, mask | bit],
                      base + place(bit), o)
        copy.start()
        right_copies[s, c, mask | bit] = copy

    parity = lax.rem(bond, 2)

    def left_part(ref, c):
        return ref.at[pl.ds(c * wide, wide)]

    left_copies, own_left = [], []
    for c in range(paints):
        for h in range(2):
            target = h * half + turn(bond // 2)
            left_copies.append((target != bond, remote(
                left_part(lt_ref, c), left_part(left_raw.at[parity], c),
                lsend.at[h, c], lrecv.at[parity, c], target, o)))
        own_left.append((lax.rem(turn(bond // 2), half) == i, pltpu.make_async_copy(
            left_part(lt_ref, c), left_part(left_raw.at[parity], c), lown.at[c])))

    lead(2.0)
    for ref, order, rank in ((right_charge_ref, order_ref, rank_ref),
                             (left_charge_ref, left_order_ref, left_rank_ref)):
        @pl.loop(0, NB)
        def _(b):
            mine = ref[b]
            total = jnp.int32(0)
            for e in range(NB):
                ahead = (ref[e] < mine) | ((ref[e] == mine) & (e < b))
                total += jnp.where(ahead, 1, 0)
            rank[b] = total

        @pl.loop(0, NB)
        def _(b):
            total = jnp.int32(0)
            for e in range(NB):
                total += jnp.where(rank[e] == b, e, 0)
            order[b] = total

    @pl.loop(0, channels)
    def _(c):
        left_shift = channel_ref[o * channels + c, 0]
        move = channel_ref[o * channels + c, 1]
        left_shift_ref[c] = lax.rem(left_shift + NQ, NQ)
        shift_ref[c] = lax.rem(left_shift + move + 2 * NQ, NQ)
        for p in range(DP):
            seen = jnp.int32(0)
            picks = [jnp.int32(0)] * most
            values = [jnp.float32(0)] * most
            for q in range(DP):
                gap = site_charges[p] - site_charges[q] - move + 4 * NQ
                allowed = lax.rem(gap, NQ) == 0
                for e in range(most):
                    here = allowed & (seen == e)
                    picks[e] = jnp.where(here, q, picks[e])
                    values[e] = jnp.where(here, operator_ref[c, p, q], values[e])
                seen += jnp.where(allowed, 1, 0)
            for e in range(most):
                site_ref[(c * DP + p) * most + e] = values[e]
                pick_ref[(c * DP + p) * most + e] = picks[e]

    @pl.loop(0, channels)
    def _(c):
        for g in range(NQ):
            bands = []
            for m in range(NPB):
                r = order_ref[g * NPB + m]
                bands.append(jnp.concatenate(
                    [rt_ref[c, r, n].astype(jnp.float32) for n in range(NPB)], 1))
            gathered[bond, c, g] = jnp.concatenate(bands, 0).astype(jnp.bfloat16)

    lead(psi_landed)
    band = i // 2 + lax.rem(i, 2) * (half // 2)
    for t in range(2):
        source = 2 * band + t
        for c in range(paints):
            @pl.when(source != bond)
            def _():
                remote(left_part(lt_ref, c), left_part(left_raw.at[t], c), lsend.at[0, c],
                       lrecv.at[t, c], source, o).wait_recv()

            @pl.when(source == bond)
            def _():
                own_left[c][1].wait()

    @pl.loop(0, NQ)
    def _(h):
        for c in range(channels):
            slot = lax.rem(h + left_shift_ref[c], NQ)
            for m in range(NPB):
                r = left_order_ref[slot * NPB + m]
                pieces = []
                for t in range(2):
                    pieces.append(jnp.concatenate(
                        [left_raw[t, c, r, n].astype(jnp.float32) for n in range(NPB)], 1))
                at = c * rows + m * sub
                left[h, at:at + sub] = jnp.concatenate(pieces, 0).astype(jnp.bfloat16)

    psi_finish()

    def left_dots(fetch, first, count):
        @pl.loop(first, first + count)
        def _(g):
            for n in range(NPB):
                terms = []
                for q in range(DP):
                    h = lax.rem(2 * NQ - site_charges[q] - g, NQ)
                    terms.append(
                        jnp.dot(left[h], fetch(q, g, n), preferred_element_type=jnp.float32)
                    )
                for q in range(DP):
                    products[q] = terms[q]
                for c in range(channels):
                    for p in range(DP):
                        total = None
                        for e in range(most):
                            at = (c * DP + p) * most + e
                            term = site_ref[at] * products[pick_ref[at], c * rows:(c + 1) * rows]
                            total = term if total is None else total + term
                        total = total.astype(jnp.bfloat16)
                        for k in range(some):
                            at = (p * some + k) * rows
                            mixed[c, g, at:at + rows, n * B:(n + 1) * B] = total[:, k * B:(k + 1) * B]

    def fetch_first(q, g, n):
        r = order_ref[g * NPB + n]
        owner = q * (NB // groups) + r // groups
        at = lax.rem(r, groups)
        t, j = owner // half, lax.rem(owner, half)
        return jnp.concatenate([
            jnp.concatenate([
                psi[j, e, k, t, pl.ds(at * tiles, tiles)].reshape(share, B) for e in range(ops)
            ], 0) for k in range(some)
        ], 1)

    slices = NQ // 2
    for g in range(slices):
        left_dots(fetch_first, g * NQ // slices, NQ // slices)
        lead(psi_landed + (g + 1) * (plan_end - psi_landed) / slices)
    lead(plan_end)
    for t in range(bits):
        pl.semaphore_signal(free_sem, inc=1, device_id=to(base + place(1 << t), o), device_id_type=MESH)
    pl.semaphore_signal(free_sem, inc=1, device_id=to(bond, other), device_id_type=MESH)

    for s in range(streams):
        for c in range(paints):
            for mask in range(half):
                right_ensure(s, c, mask)
    for copy in right_exchange:
        copy.wait_send()
    for copy in right_copies.values():
        copy.wait_send()
    for away_from_here, copy in left_copies:
        @pl.when(away_from_here)
        def _():
            copy.wait_send()

    def right_dots(g):
        total = None
        for c in range(channels):
            source = lax.rem(g + shift_ref[c], NQ)
            term = lax.dot_general(
                mixed[c, source], right[c, g], (((1,), (1,)), ((), ())),
                preferred_element_type=jnp.float32,
            )
            total = term if total is None else total + term
        return total

    own_half = DP // ops * some * rows

    @pl.loop(0, NQ)
    def _(g):
        for c in range(channels):
            for u in range(bonds // 2):
                pair = [gathered[2 * u + t, c, g].astype(jnp.float32) for t in range(2)]
                for m in range(NPB):
                    at = m * B + u * sub
                    right[c, g, at:at + sub] = jnp.concatenate(
                        [x[m * fine:(m + 1) * fine] for x in pair], 0).astype(jnp.bfloat16)
        total = right_dots(g)
        for e in range(ops):
            part_sum[g, e] = total[e * own_half:(e + 1) * own_half]
        remote(part_sum.at[g, other], got_first.at[g], osend.at[g], orecv.at[g], bond, other).start()

    span = NB // streams

    def spot_of(s, m):
        return (s // span * NPB + m) * span + lax.rem(s, span)

    def view_second(j, c, s):
        return psi.at[j, o, c, :, pl.ds(s * NPB * span, NPB * span)]

    pl.semaphore_wait(free_sem, bits + 1)

    @pl.loop(0, NQ)
    def _(g):
        remote(part_sum.at[g, other], got_first.at[g], osend.at[g], orecv.at[g], bond, other).wait()
        total = (part_sum[g, o] + got_first[g]).astype(jnp.bfloat16)
        for p in range(DP // ops):
            for k in range(some):
                for m in range(NPB):
                    at = ((p * some + k) * NPB + m) * sub
                    for n in range(NPB):
                        psi[i, o, k, p, spot_of(g * NPB + n, m)] = total[at:at + sub, n * B:(n + 1) * B]

    unused, again_step, again_arrive, again_finish = spread(view_second, [], [turns, turns])
    for n in range(bits):
        again_step(0, n)
        again_step(1, n)
    again_arrive(0)

    def slot_of(x):
        return lax.rem(2 * x, half) + (2 * x) // half if not isinstance(x, int) else (2 * x) % half + (2 * x) // half

    def fetch_second(q, g, n):
        per = DP // ops
        return jnp.concatenate([
            jnp.concatenate([
                psi[slot_of(x), q // per, k, q % per, spot_of(g * NPB + n, m)]
                for m in range(NPB) for x in range(half)
            ], 0) for k in range(some)
        ], 1)

    holder = turn(i)
    trades = []

    def start_trade(s):
        wanted = psi.at[holder, o, :, :, pl.ds(s * NPB * span + (1 - part) * span, span)]
        trades.append(remote(wanted, swap.at[s], wsend.at[s], wrecv.at[s], partner, o))
        trades[-1].start()

    start_trade(0)
    left_dots(fetch_second, 0, NQ // streams)
    again_finish()
    start_trade(1)
    left_dots(fetch_second, NQ // streams, NQ // streams)

    @pl.loop(0, NQ)
    def _(g):
        total = right_dots(g)
        for x in range(DP * some):
            for m in range(NPB):
                at = x * rows + m * sub
                part_sum[g, m, x * sub:(x + 1) * sub] = total[at:at + sub]
        remote(part_sum.at[g, other], got_second.at[g], osend2.at[g], orecv2.at[g], bond, other).start()

    @pl.loop(0, NQ)
    def _(g):
        remote(part_sum.at[g, other], got_second.at[g], osend2.at[g], orecv2.at[g], bond, other).wait()
        total = (part_sum[g, o] + got_second[g]).astype(jnp.bfloat16)
        for n in range(NPB):
            for x in range(DP * some):
                sorted_out[g * NPB + n, x] = total[x * sub:(x + 1) * sub, n * B:(n + 1) * B]

    for r in range(NB):
        s = rank_ref[r]
        for p in range(DP):
            for k in range(some):
                ready[p * (NB // groups) + r // groups, k, r % groups] = sorted_out[s, p * some + k]

    sends = []
    for e in range(1, bonds):
        target = lax.rem(bond + e, bonds)
        copy = remote(ready.at[target], landed.at[bond], asend.at[e], arecv.at[e], target, o)
        copy.start()
        sends.append(copy)

    for copy in trades:
        copy.wait()
    for p in range(DP // ops):
        for r in range(NB):
            s = rank_ref[r]
            for k in range(some):
                cols = slice((p * NB + r) * B, (p * NB + r + 1) * B)
                one_ref[part * some + k, :, cols] = psi[
                    holder, o, k, p, spot_of(s, part)].astype(jnp.float32)
                one_ref[(1 - part) * some + k, :, cols] = swap[s // span, k, p, lax.rem(s, span)].astype(jnp.float32)

    landed[bond] = ready[bond]
    for copy in sends:
        copy.wait()
    for s in range(bonds):
        x = s % half
        spot = x // 2 + (x % 2) * (half // 2)
        for k in range(some):
            for at in range(groups):
                two_ref[(s // half) * some + k, spot * sub:(spot + 1) * sub, at * B:(at + 1) * B] = (
                    landed[s, k, at].astype(jnp.float32))


def whole(wave, left_tiles, right_tiles, tables, bonds, ops):
    roots, sector_rows, strip = wave.shape
    channels = left_tiles.shape[0]
    half = bonds // 2
    bits = half.bit_length() - 1
    some = roots // 2
    fine = left_tiles.shape[3]
    sub = 2 * fine
    rows = NPB * sub
    share = sector_rows // ops
    groups = strip // B
    height = DP * some * rows
    paints = 4
    vmem = pl.BlockSpec(memory_space=pltpu.VMEM)
    smem = pl.BlockSpec(memory_space=pltpu.SMEM)
    dma = pltpu.SemaphoreType.DMA
    bf, f32 = jnp.bfloat16, jnp.float32
    return pl.pallas_call(
        functools.partial(whole_kernel, half, ops, some, channels, site_charge_table),
        out_shape=[
            jax.ShapeDtypeStruct((roots, NPB * B // bonds, DP // ops * NB * B), f32),
            jax.ShapeDtypeStruct((roots, share, strip), f32),
        ],
        in_specs=[smem] * 4 + [pl.BlockSpec(memory_space=pl.ANY), vmem, vmem],
        out_specs=[vmem, vmem],
        scratch_shapes=[pltpu.SMEM((NB,), jnp.int32)] * 4 + [pltpu.SMEM((channels,), jnp.int32)] * 2 + [
            pltpu.SMEM((channels * DP * DP,), f32), pltpu.SMEM((channels * DP * DP,), jnp.int32),
            pltpu.VMEM((DP, channels * rows, some * B), f32),
            pltpu.VMEM((half, ops, some, 2, groups * share // sub, sub, B), bf),
            pltpu.VMEM((bonds, channels, NQ, NPB * fine, NPB * B), bf),
            pltpu.VMEM((channels, NQ, NPB * B, NPB * B), bf),
            pltpu.VMEM((NQ, channels * rows, NPB * B), bf),
            pltpu.VMEM((2,) + left_tiles.shape, bf),
            pltpu.VMEM((channels, NQ, height, NPB * B), bf),
            pltpu.VMEM((NQ, ops, height // ops, NPB * B), f32),
            pltpu.VMEM((NQ, height // ops, NPB * B), f32),
            pltpu.VMEM((NQ, height // ops, NPB * B), f32),
            pltpu.VMEM((roots, share, strip), f32),
            pltpu.VMEM((some, groups * share // sub, sub, B), bf),
            pltpu.VMEM((2, some, DP // ops, NB // 2, sub, B), bf),
            pltpu.VMEM((NB, DP * some, sub, B), bf),
            pltpu.VMEM((bonds, some, groups, sub, B), bf),
            pltpu.VMEM((bonds, some, groups, sub, B), bf),
            dma, dma((some,)), dma((some,)),
            dma((2, some, half)), dma((2, some, half)), dma((2, some, half)), dma((2, some, half)),
            dma((paints,)), dma((paints,)), dma((2, paints, half)), dma((2, paints, half)),
            dma((2, paints)), dma((2, paints)), dma((paints,)),
            dma((NQ,)), dma((NQ,)), dma((NQ,)), dma((NQ,)),
            dma((2,)), dma((2,)), dma((bonds,)), dma((bonds,)),
            pltpu.SemaphoreType.REGULAR,
        ],
        compiler_params=pltpu.CompilerParams(
            collective_id=3, has_side_effects=True, vmem_limit_bytes=67043328
        ),
        name="whole",
    )(*tables, wave, left_tiles, right_tiles)


def local_whole(
    wavefunction, left_tiles, right_tiles, site_operators, left_charge, right_charge, channel_charge
):
    tables = (left_charge, right_charge, channel_charge, site_operators)
    return tuple(whole(
        wavefunction, left_tiles, right_tiles, tables, lax.axis_size("bond"), lax.axis_size("op")
    ))


def fits(mesh, wavefunction, left_tiles):
    bonds, ops = mesh.shape["bond"], mesh.shape["op"]
    strip = wavefunction.shape[2] // bonds
    fine = left_tiles.shape[3] // bonds
    channels = left_tiles.shape[0] // ops
    return (
        ops == NPB and bonds == NB and strip % B == 0 and 2 * fine * (bonds // 2) == B
        and channels % 4 == 0 and NPB * fine == 16
    )


def local(
    wavefunction, left_tiles, right_tiles, site_operators, left_charge, right_charge, channel_charge
):
    bonds = lax.axis_size("bond")
    ops = lax.axis_size("op")
    bond = lax.axis_index("bond")
    op = lax.axis_index("op")
    roots, sector_rows, strip = wavefunction.shape
    channels = site_operators.shape[0]
    half = bonds // 2
    part = bond // half
    some = roots // 2
    chunk = left_tiles.shape[3]
    band = 2 * chunk
    rows = NPB * band
    held = -(-rows // 16) * 16
    width = min(strip, B)
    groups = strip // width
    own_charge = lax.dynamic_slice_in_dim(channel_charge, op * channels, channels, 0)
    left_order = jnp.argsort(left_charge, stable=True).astype(jnp.int32)
    right_order = jnp.argsort(right_charge, stable=True).astype(jnp.int32)
    shift = (own_charge[:, 0] + own_charge[:, 1]) % NQ
    site = site_masks(site_operators, own_charge).reshape(-1)

    right = right_tiles[:, right_order].transpose(0, 1, 3, 2, 4).reshape(
        channels, NB, chunk, NPB * B
    )
    right = lax.all_gather(right, "bond", axis=2, tiled=True).reshape(
        channels, NQ, NPB * B, NPB * B
    )

    even = [(b, b // 2 + (b % 2) * half) for b in range(bonds)]
    odd = [(b, b // 2 + (1 - b % 2) * half) for b in range(bonds)]
    one = lax.ppermute(left_tiles, "bond", even)
    two = lax.ppermute(left_tiles, "bond", odd)
    low = jnp.where(part == 0, one, two)
    high = jnp.where(part == 0, two, one)
    left = jnp.concatenate([low, high], axis=3)
    left_slots = ((jnp.arange(NQ)[:, None] + own_charge[None, :, 0]) % NQ)[:, :, None] * NPB + jnp.arange(NPB)
    left = left[jnp.arange(channels)[None, :, None], left_order[left_slots]]
    left = left.transpose(0, 1, 2, 4, 3, 5).reshape(NQ, channels, rows, NPB * B)
    left = jnp.pad(left, ((0, 0), (0, 0), (0, held - rows), (0, 0)))
    left = left.reshape(NQ, channels * held, NPB * B)

    share = sector_rows // ops
    psi = lax.dynamic_slice_in_dim(wavefunction, op * share, share, 1).astype(jnp.bfloat16)
    psi = psi.reshape(2, some, share, groups, width).transpose(0, 1, 3, 2, 4)
    kept = lax.dynamic_index_in_dim(psi, part, 0, keepdims=False)
    other = lax.dynamic_index_in_dim(psi, 1 - part, 0, keepdims=False)
    (psi,) = spread(kept, other, half, ops, True)

    def load_whole(ref, block):
        return ref[block]

    def load_first(ref, block):
        owner = block // groups
        t, j, at = owner // half, lax.rem(owner, half), lax.rem(block, groups)
        return jnp.concatenate(
            [jnp.concatenate([ref[j, o, t, k, at] for o in range(ops)], 0) for k in range(some)], 1
        )

    load = load_first
    if width < B:
        psi = psi.reshape(half, ops, 2, some, share, strip).transpose(2, 0, 5, 1, 4, 3)
        psi = psi.reshape(DP * NB, B, sector_rows, some).transpose(0, 2, 3, 1)
        psi = psi.reshape(DP * NB, sector_rows, some * B)
        load = load_whole
    elif share % 16:
        psi = psi.transpose(2, 0, 4, 1, 5, 3, 6).reshape(DP * NB, sector_rows, some * B)
        load = load_whole

    def unpack(result):
        result = result.reshape(NB, DP, some, held, B)[:, :, :, :rows]
        return result.reshape(NB, DP, some, NPB, band, B)

    def summed_share(parts, axis):
        size = parts.shape[axis] // ops
        total = lax.dynamic_slice_in_dim(parts, op * size, size, axis)
        for e in range(1, ops):
            to = (op + e) % ops
            sent = lax.dynamic_slice_in_dim(parts, to * size, size, axis)
            total += lax.ppermute(sent, "op", [(o, (o + e) % ops) for o in range(ops)])
        return total

    first = unpack(apply_all(right_order, shift, site, psi, left, right, held, some, load))
    turned = (DP * NB, some, NPB, band, B)
    if DP % ops == 0:
        first = summed_share(first, 1).transpose(1, 0, 2, 3, 4, 5)
        first = first.reshape((DP * NB // ops,) + turned[1:])
    else:
        first = summed_share(first.transpose(1, 0, 2, 3, 4, 5).reshape(turned), 0)
    blocks = first.shape[0]

    mine = lax.dynamic_index_in_dim(first, part, 2, keepdims=False)
    theirs = lax.dynamic_index_in_dim(first, 1 - part, 2, keepdims=False)
    again = first.astype(jnp.bfloat16).transpose(1, 0, 2, 3, 4)
    again, back = spread(again, theirs.astype(jnp.bfloat16), half, ops, False)
    back = back.astype(jnp.float32)
    both = jnp.stack([jnp.where(part == 0, mine, back), jnp.where(part == 0, back, mine)])
    sigma_one = both.transpose(0, 2, 3, 1, 4).reshape(roots, band, blocks * B)

    def load_second(ref, block):
        o, at = block // blocks, lax.rem(block, blocks)
        return jnp.concatenate(
            [
                jnp.concatenate([ref[j, o, 0, k, at, m] for m in range(NPB) for j in range(half)], 0)
                for k in range(some)
            ], 1,
        )

    load = load_second
    if band % 16:
        again = again[:, :, 0].transpose(1, 3, 4, 0, 5, 2, 6)
        again = again.reshape(DP * NB, sector_rows, some * B)
        load = load_whole
    second = unpack(apply_all(right_order, shift, site, again, left, right, held, some, load))
    if ops == NPB:
        second = summed_share(second, 3)
    else:
        second = lax.psum(second, "op")
    tiles = second.shape[3]
    second = second.astype(jnp.bfloat16).transpose(2, 3, 4, 1, 0, 5)
    second = second.reshape(some, tiles * band, bonds, strip).transpose(2, 0, 1, 3)
    second = lax.all_to_all(second, "bond", split_axis=0, concat_axis=0, tiled=True)
    second = second.reshape(2, half, some, tiles, band, strip).transpose(0, 2, 3, 1, 4, 5)
    second = second.reshape(roots, tiles * B, strip).astype(jnp.float32)
    if ops != NPB:
        second = lax.dynamic_slice_in_dim(second, op * share, share, 1)
    return (sigma_one, second)


def solution(mesh):
    def run(*args):
        body = local_whole if fits(mesh, args[0], args[1]) else local
        return jax.shard_map(
            body,
            mesh=mesh,
            in_specs=(
                P(None, None, "bond"),
                P("op", None, None, "bond", None),
                P("op", None, None, "bond", None),
                P("op", None, None),
                P(),
                P(),
                P(),
            ),
            out_specs=(P(None, "bond", "op"), P(None, "op", "bond")),
            check_vma=False,
        )(*args)

    return run
```

```python
import functools

import jax
import jax.numpy as jnp
from jax import lax
from jax.experimental import pallas as pl
from jax.experimental.pallas import tpu as pltpu
from jax.sharding import PartitionSpec as P

M = 2048
B = 128
NQ = 8
DP = 4
NB = 16
NPB = 2

site_charge_table = (0, 1, 1, 2)
MESH = pl.DeviceIdType.MESH


def site_masks(site_operators, channel_charge):
    site_charge = jnp.array(site_charge_table, dtype=jnp.int32)
    charge_step = site_charge[:, None] - site_charge[None, :]
    allowed = (charge_step[None, :, :] - channel_charge[:, 1][:, None, None]) % NQ == 0
    return jnp.where(allowed, site_operators, jnp.zeros_like(site_operators))


def spread_kernel(half, ops, colours, first, *refs):
    if first:
        x_ref, y_ref, g_ref = refs[:3]
        z_ref = None
        scratch = refs[3:]
    else:
        x_ref, y_ref, g_ref, z_ref = refs[:4]
        scratch = refs[4:]
    own_sem, psend, precv, send_sem, recv_sem, fsend, frecv = scratch
    bond = lax.axis_index("bond")
    o = lax.axis_index("op")
    i = lax.rem(bond, half)
    part = bond // half
    base = bond - i
    partner = i + half * (1 - part)
    bits = half.bit_length() - 1
    streams = 2 if first else 1

    def place(mask):
        at = i
        for t in range(bits):
            if mask >> t & 1:
                at = at + (1 << t) * (1 - 2 * lax.rem(i // (1 << t), 2))
        return at

    def to(bond_index, op_index):
        return {"bond": bond_index, "op": op_index}

    barrier = pltpu.get_barrier_semaphore()
    for t in range(bits):
        pl.semaphore_signal(
            barrier, inc=1, device_id=to(base + place(1 << t), o), device_id_type=MESH
        )
    pl.semaphore_signal(barrier, inc=1, device_id=to(partner, o), device_id_type=MESH)
    for e in range(1, ops):
        pl.semaphore_signal(
            barrier, inc=1, device_id=to(bond, lax.rem(o + e, ops)), device_id_type=MESH
        )
    pl.semaphore_wait(barrier, bits + ops)

    index = (part, 1 - part) if first else (0,)
    exchange = []
    for c in range(colours if first else 1):
        exchange.append(pltpu.make_async_remote_copy(
            src_ref=y_ref.at[c] if first else y_ref,
            dst_ref=g_ref.at[i, o, part, c] if first else z_ref,
            send_sem=psend.at[c], recv_sem=precv.at[c],
            device_id=to(partner, o), device_id_type=MESH,
        ))
        exchange[-1].start()

    copies = {}
    forwards = []
    ready = set()

    def block(s, c, mask):
        if s == 0 and mask == 0:
            return x_ref.at[c]
        return g_ref.at[place(mask), o, index[s], c]

    def ensure(s, c, mask):
        if (s, c, mask) in ready:
            return
        ready.add((s, c, mask))
        if mask:
            copies[s, c, mask].wait_recv()
        elif s == 1:
            exchange[c].wait_recv()
        for e in range(1, ops):
            copy = pltpu.make_async_remote_copy(
                src_ref=block(s, c, mask), dst_ref=g_ref.at[place(mask), o, index[s], c],
                send_sem=fsend.at[s, c, mask, e], recv_sem=frecv.at[s, c, mask, e],
                device_id=to(bond, lax.rem(o + e, ops)), device_id_type=MESH,
            )
            copy.start()
            forwards.append(copy)

    own = pltpu.make_async_copy(x_ref, g_ref.at[i, o, index[0]], own_sem)
    own.start()
    for s in range(streams):
        reached = [[0] for c in range(colours)]
        for step in range(bits):
            for at in range(max(len(r) for r in reached)):
                for c in range(colours):
                    mask = reached[c][at]
                    bit = 1 << (c + step) % bits
                    ensure(s, c, mask)
                    copy = pltpu.make_async_remote_copy(
                        src_ref=block(s, c, mask), dst_ref=g_ref.at[place(mask), o, index[s], c],
                        send_sem=send_sem.at[s, c, mask | bit], recv_sem=recv_sem.at[s, c, mask | bit],
                        device_id=to(base + place(bit), o), device_id_type=MESH,
                    )
                    copy.start()
                    copies[s, c, mask | bit] = copy
            for c in range(colours):
                bit = 1 << (c + step) % bits
                reached[c] = reached[c] + [mask | bit for mask in reached[c]]
    for s in range(streams):
        for mask in range(half):
            for c in range(colours):
                ensure(s, c, mask)
    own.wait()
    for copy in copies.values():
        copy.wait_send()
    for copy in exchange:
        copy.wait_send()
        if not first:
            copy.wait_recv()
    for copy in forwards:
        copy.wait()


def spread(x, y, half, ops, first):
    colours = x.shape[0]
    streams = 2 if first else 1
    shapes = [jax.ShapeDtypeStruct((half, ops, streams) + x.shape, x.dtype)]
    if not first:
        shapes.append(jax.ShapeDtypeStruct(y.shape, y.dtype))
    size = x.size * half * ops * streams * 2
    return pl.pallas_call(
        functools.partial(spread_kernel, half, ops, colours, first),
        out_shape=shapes,
        in_specs=[pl.BlockSpec(memory_space=pltpu.VMEM)] * 2,
        out_specs=[pl.BlockSpec(memory_space=pl.ANY)] * len(shapes),
        scratch_shapes=[
            pltpu.SemaphoreType.DMA,
            pltpu.SemaphoreType.DMA((colours,)),
            pltpu.SemaphoreType.DMA((colours,)),
            pltpu.SemaphoreType.DMA((streams, colours, half)),
            pltpu.SemaphoreType.DMA((streams, colours, half)),
            pltpu.SemaphoreType.DMA((streams, colours, half, ops)),
            pltpu.SemaphoreType.DMA((streams, colours, half, ops)),
        ],
        compiler_params=pltpu.CompilerParams(
            collective_id=1 if first else 2, has_side_effects=True
        ),
        cost_estimate=pl.CostEstimate(flops=0, bytes_accessed=16 * size, transcendentals=0),
        name="spread_first" if first else "spread_second",
    )(x, y)


def apply_kernel(
    channels, rows, roots, site_charges, load,
    order_ref, shift_ref, site_ref, psi_ref, left_ref, right_ref, out_ref, mixed
):
    @pl.loop(0, NQ)
    def _(g):
        for n in range(NPB):
            r = order_ref[g * NPB + n]
            terms = []
            for q in range(DP):
                h = lax.rem(2 * NQ - site_charges[q] - g, NQ)
                terms.append(
                    jnp.dot(left_ref[h], load(psi_ref, q * NB + r), preferred_element_type=jnp.float32)
                )
            for c in range(channels):
                for p in range(DP):
                    total = site_ref[(c * DP + p) * DP] * terms[0][c * rows:(c + 1) * rows]
                    for q in range(1, DP):
                        total += site_ref[(c * DP + p) * DP + q] * terms[q][c * rows:(c + 1) * rows]
                    total = total.astype(jnp.bfloat16)
                    for k in range(roots):
                        at = (p * roots + k) * rows
                        mixed[c, g, at:at + rows, n * B:(n + 1) * B] = total[:, k * B:(k + 1) * B]

    @pl.loop(0, NQ)
    def _(g):
        total = None
        for c in range(channels):
            source = lax.rem(g + shift_ref[c], NQ)
            term = lax.dot_general(
                mixed[c, source], right_ref[c, g], (((1,), (1,)), ((), ())),
                preferred_element_type=jnp.float32,
            )
            total = term if total is None else total + term
        for m in range(NPB):
            out_ref[order_ref[g * NPB + m]] = total[:, m * B:(m + 1) * B]


def apply_all(order, shift, site, psi, left, right, rows, roots, load):
    channels = right.shape[0]
    height = DP * roots * rows
    smem = pl.BlockSpec(memory_space=pltpu.SMEM)
    vmem = pl.BlockSpec(memory_space=pltpu.VMEM)
    return pl.pallas_call(
        functools.partial(apply_kernel, channels, rows, roots, site_charge_table, load),
        out_shape=jax.ShapeDtypeStruct((NB, height, B), jnp.float32),
        in_specs=[smem, smem, smem, vmem, vmem, vmem],
        out_specs=vmem,
        scratch_shapes=[pltpu.VMEM((channels, NQ, height, NPB * B), jnp.bfloat16)],
        compiler_params=pltpu.CompilerParams(vmem_limit_bytes=58 * 1024 * 1024),
        name="apply_all",
    )(order, shift, site, psi, left, right)


def timetable(bits, psi_orders, right_orders, psi_parts, left_parts, slot, delay, prepared):
    orders = {"psi": psi_orders, "right": right_orders}
    waiting, done = [], []
    landed = 0.0

    def open_node(family, s, c, mask, level, at):
        for n in range(level, bits):
            waiting.append((family, s, c, mask, n, at))

    for c in range(len(psi_orders[0])):
        open_node("psi", 0, c, 0, 0, 0.0)
    for c in range(len(right_orders[0])):
        open_node("right", 0, c, 0, 0, prepared)
    far = [("psi", c) for c in range(psi_parts)] + [("left", c) for c in range(left_parts)]
    far += [("right", c) for c in range(len(right_orders[0]))]
    free = [0.0] * bits
    far_free, now = 0.0, 0.0
    while waiting or far:
        for link in range(bits):
            if free[link] > now:
                continue
            if link == bits - 1 and far and far_free <= now:
                kind, c = far.pop(0)
                if kind != "right" or now >= prepared:
                    done.append((now, ("far", kind, c, 0)))
                    done.append((now + slot, ("far", kind, c, 1)))
                    free[link] = now + slot
                    far_free = now + 2 * slot
                    if kind != "left":
                        open_node(kind, 1, c, 0, 0, now + 2 * slot + 2 * delay)
                    continue
                far.insert(0, (kind, c))
            best = None
            for item in waiting:
                family, s, c, mask, n, at = item
                if orders[family][s][c][n] != link or at > now:
                    continue
                key = (family == "right", n - bits if n < bits - 1 else 0, n, at, s, c, mask)
                if best is None or key < best[0]:
                    best = (key, item)
            if best is None:
                continue
            family, s, c, mask, n, at = best[1]
            waiting.remove(best[1])
            done.append((now, ("hop", family, s, c, mask, n)))
            free[link] = now + slot
            arrival = now + slot + delay
            if family == "psi":
                landed = max(landed, arrival)
            open_node(family, s, c, mask | 1 << link, n + 1, arrival)
        now += slot / 16
    done.sort(key=lambda entry: entry[0])
    return done, landed, now + slot


def whole_kernel(
    half, ops, some, channels, site_charges,
    left_charge_ref, right_charge_ref, channel_ref, operator_ref,
    wave_ref, lt_ref, rt_ref, one_ref, two_ref,
    order_ref, rank_ref, left_order_ref, left_rank_ref, shift_ref, left_shift_ref, site_ref,
    psi, gathered, right, left, left_raw, mixed, part_sum, got_first, got_second, stage, away,
    swap, sorted_out, ready, landed,
    stage_sem, psend, precv, send_sem, recv_sem, fsend, frecv,
    rpsend, rprecv, rsend, rrecv, lsend, lrecv, lown, osend, orecv, osend2, orecv2,
    wsend, wrecv, asend, arecv, free_sem,
):
    bond = lax.axis_index("bond")
    o = lax.axis_index("op")
    bonds = 2 * half
    i = lax.rem(bond, half)
    part = bond // half
    base = bond - i
    partner = i + half * (1 - part)
    bits = half.bit_length() - 1
    rows = left.shape[1] // channels
    sub = rows // NPB
    fine = lt_ref.shape[3]
    streams = 2
    other = lax.rem(o + 1, ops)

    def place(mask):
        at = i
        for t in range(bits):
            if mask >> t & 1:
                at = at + (1 << t) * (1 - 2 * lax.rem(i // (1 << t), 2))
        return at

    def turn(x):
        return lax.rem(2 * x, half) + (2 * x) // half

    def to(bond_index, op_index):
        return {"bond": bond_index, "op": op_index}

    def remote(src, dst, send, recv, bond_index, op_index):
        return pltpu.make_async_remote_copy(
            src_ref=src, dst_ref=dst, send_sem=send, recv_sem=recv,
            device_id=to(bond_index, op_index), device_id_type=MESH,
        )

    barrier = pltpu.get_barrier_semaphore()
    for e in range(1, bonds):
        pl.semaphore_signal(
            barrier, inc=1, device_id=to(lax.rem(bond + e, bonds), o), device_id_type=MESH
        )
    pl.semaphore_signal(barrier, inc=1, device_id=to(bond, other), device_id_type=MESH)

    share = stage.shape[1]
    groups = stage.shape[2] // B
    load = pltpu.make_async_copy(wave_ref.at[:, pl.ds(o * share, share), :], stage, stage_sem)
    load.start()
    load.wait()
    tiles = share // sub
    for k in range(some):
        for at in range(groups):
            for t in range(tiles):
                psi[i, o, k, part, at * tiles + t] = stage[
                    part * some + k, t * sub:(t + 1) * sub, at * B:(at + 1) * B
                ].astype(jnp.bfloat16)
                away[k, at * tiles + t] = stage[
                    (1 - part) * some + k, t * sub:(t + 1) * sub, at * B:(at + 1) * B
                ].astype(jnp.bfloat16)
    pl.semaphore_wait(barrier, bonds)

    def spread(view, exchange, orders):
        colours = some
        copies, forwards, ready_set = {}, [[], []], set()

        def slot(s, c, mask):
            return view(place(mask), c, s)

        def ensure(s, c, mask):
            if (s, c, mask) in ready_set:
                return
            ready_set.add((s, c, mask))
            if mask:
                copies[s, c, mask].wait_recv()
            elif s == 1 and exchange:
                exchange[c].wait_recv()
            copy = remote(slot(s, c, mask), slot(s, c, mask), fsend.at[s, c, mask],
                          frecv.at[s, c, mask], bond, other)
            copy.start()
            forwards[s].append(copy)

        def hop(s, c, mask, n):
            bit = 1 << orders[s][c][n]
            ensure(s, c, mask)
            copy = remote(slot(s, c, mask), slot(s, c, mask), send_sem.at[s, c, mask | bit],
                          recv_sem.at[s, c, mask | bit], base + place(bit), o)
            copy.start()
            copies[s, c, mask | bit] = copy

        def step(s, n):
            for at in range(1 << n):
                for c in range(colours):
                    hop(s, c, sum(1 << orders[s][c][b] for b in range(n) if at >> b & 1), n)

        def arrive(s):
            for mask in range(half):
                for c in range(colours):
                    ensure(s, c, mask)
            while forwards[s]:
                forwards[s].pop().wait()

        def finish():
            for s in range(streams):
                arrive(s)
            for copy in copies.values():
                copy.wait_send()
            for copy in exchange:
                copy.wait_send()

        return hop, step, arrive, finish

    exchange = []
    for c in range(some):
        exchange.append(remote(away.at[c], psi.at[i, o, c, part], psend.at[c], precv.at[c], partner, o))
    last = bits - 1
    turns = [(0, 1, last), (1, last, 0), (last, 0, 1)]
    psi_orders = [turns, [(0, last, 1), (1, last, 0), (last, 1, 0)]]
    right_orders = [[(last, 0, 1), (last, 1, 0), (0, last, 1), (1, last, 0)]] * 2
    paints = len(right_orders[0])
    wide = channels // paints
    def view_first(j, c, s):
        return psi.at[j, o, c, part if s == 0 else 1 - part]

    psi_hop, unused, unused, psi_finish = spread(view_first, exchange, psi_orders)
    plan, psi_landed, plan_end = timetable(
        bits, psi_orders, right_orders, some, paints, 2.8, 1.5, 6.0)
    plan = list(plan)

    def lead(until):
        while plan and plan[0][0] <= until:
            operation = plan.pop(0)[1]
            if operation[0] == "far":
                send_far(*operation[1:])
            elif operation[1] == "psi":
                psi_hop(*operation[2:])
            else:
                right_hop(*operation[2:])

    def send_far(kind, c, turn_of):
        if kind == "psi":
            item = [(None, exchange[c])]
        elif kind == "right":
            item = [(None, right_exchange[c])]
        else:
            item = left_copies[2 * c:2 * c + 2] + own_left[c:c + 1]
        ready_now = lax.rem(part + i // (half // 2), 2) == turn_of
        for when, copy in item:
            @pl.when(ready_now if when is None else when & ready_now)
            def _():
                copy.start()

    def tile(slot, c):
        return gathered.at[slot, pl.ds(c * wide, wide)]

    right_exchange = []
    for c in range(paints):
        right_exchange.append(remote(tile(bond, c), tile(bond, c), rpsend.at[c], rprecv.at[c], partner, o))
    right_copies, right_ready = {}, set()

    def right_ensure(s, c, mask):
        if (s, c, mask) in right_ready:
            return
        right_ready.add((s, c, mask))
        if mask:
            right_copies[s, c, mask].wait_recv()
        elif s == 1:
            right_exchange[c].wait_recv()

    def right_hop(s, c, mask, n):
        start = base if s == 0 else half - base
        bit = 1 << right_orders[s][c][n]
        right_ensure(s, c, mask)
        here = tile(start + place(mask), c)
        copy = remote(here, here, rsend.at[s, c, mask | bit], rrecv.at[s, c, mask | bit],
                      base + place(bit), o)
        copy.start()
        right_copies[s, c, mask | bit] = copy

    parity = lax.rem(bond, 2)

    def left_part(ref, c):
        return ref.at[pl.ds(c * wide, wide)]

    left_copies, own_left = [], []
    for c in range(paints):
        for h in range(2):
            target = h * half + turn(bond // 2)
            left_copies.append((target != bond, remote(
                left_part(lt_ref, c), left_part(left_raw.at[parity], c),
                lsend.at[h, c], lrecv.at[parity, c], target, o)))
        own_left.append((lax.rem(turn(bond // 2), half) == i, pltpu.make_async_copy(
            left_part(lt_ref, c), left_part(left_raw.at[parity], c), lown.at[c])))

    lead(2.0)
    for ref, order, rank in ((right_charge_ref, order_ref, rank_ref),
                             (left_charge_ref, left_order_ref, left_rank_ref)):
        @pl.loop(0, NB)
        def _(b):
            mine = ref[b]
            total = jnp.int32(0)
            for e in range(NB):
                ahead = (ref[e] < mine) | ((ref[e] == mine) & (e < b))
                total += jnp.where(ahead, 1, 0)
            rank[b] = total

        @pl.loop(0, NB)
        def _(b):
            total = jnp.int32(0)
            for e in range(NB):
                total += jnp.where(rank[e] == b, e, 0)
            order[b] = total

    @pl.loop(0, channels)
    def _(c):
        left_shift = channel_ref[o * channels + c, 0]
        move = channel_ref[o * channels + c, 1]
        left_shift_ref[c] = lax.rem(left_shift + NQ, NQ)
        shift_ref[c] = lax.rem(left_shift + move + 2 * NQ, NQ)
        for p in range(DP):
            for q in range(DP):
                gap = site_charges[p] - site_charges[q] - move + 4 * NQ
                site_ref[(c * DP + p) * DP + q] = jnp.where(
                    lax.rem(gap, NQ) == 0, operator_ref[c, p, q], 0.0)

    @pl.loop(0, channels)
    def _(c):
        for g in range(NQ):
            bands = []
            for m in range(NPB):
                r = order_ref[g * NPB + m]
                bands.append(jnp.concatenate(
                    [rt_ref[c, r, n].astype(jnp.float32) for n in range(NPB)], 1))
            gathered[bond, c, g] = jnp.concatenate(bands, 0).astype(jnp.bfloat16)

    lead(psi_landed)
    band = i // 2 + lax.rem(i, 2) * (half // 2)
    for t in range(2):
        source = 2 * band + t
        for c in range(paints):
            @pl.when(source != bond)
            def _():
                remote(left_part(lt_ref, c), left_part(left_raw.at[t], c), lsend.at[0, c],
                       lrecv.at[t, c], source, o).wait_recv()

            @pl.when(source == bond)
            def _():
                own_left[c][1].wait()

    @pl.loop(0, NQ)
    def _(h):
        for c in range(channels):
            slot = lax.rem(h + left_shift_ref[c], NQ)
            for m in range(NPB):
                r = left_order_ref[slot * NPB + m]
                pieces = []
                for t in range(2):
                    pieces.append(jnp.concatenate(
                        [left_raw[t, c, r, n].astype(jnp.float32) for n in range(NPB)], 1))
                at = c * rows + m * sub
                left[h, at:at + sub] = jnp.concatenate(pieces, 0).astype(jnp.bfloat16)

    psi_finish()

    def left_dots(fetch, first, count):
        @pl.loop(first, first + count)
        def _(g):
            for n in range(NPB):
                terms = []
                for q in range(DP):
                    h = lax.rem(2 * NQ - site_charges[q] - g, NQ)
                    terms.append(
                        jnp.dot(left[h], fetch(q, g, n), preferred_element_type=jnp.float32)
                    )
                for c in range(channels):
                    for p in range(DP):
                        total = site_ref[(c * DP + p) * DP] * terms[0][c * rows:(c + 1) * rows]
                        for q in range(1, DP):
                            total += site_ref[(c * DP + p) * DP + q] * terms[q][c * rows:(c + 1) * rows]
                        total = total.astype(jnp.bfloat16)
                        for k in range(some):
                            at = (p * some + k) * rows
                            mixed[c, g, at:at + rows, n * B:(n + 1) * B] = total[:, k * B:(k + 1) * B]

    def fetch_first(q, g, n):
        r = order_ref[g * NPB + n]
        owner = q * (NB // groups) + r // groups
        at = lax.rem(r, groups)
        t, j = owner // half, lax.rem(owner, half)
        return jnp.concatenate([
            jnp.concatenate([
                psi[j, e, k, t, pl.ds(at * tiles, tiles)].reshape(share, B) for e in range(ops)
            ], 0) for k in range(some)
        ], 1)

    slices = NQ // 2
    for g in range(slices):
        left_dots(fetch_first, g * NQ // slices, NQ // slices)
        lead(psi_landed + (g + 1) * (plan_end - psi_landed) / slices)
    lead(plan_end)
    for t in range(bits):
        pl.semaphore_signal(free_sem, inc=1, device_id=to(base + place(1 << t), o), device_id_type=MESH)
    pl.semaphore_signal(free_sem, inc=1, device_id=to(bond, other), device_id_type=MESH)

    for s in range(streams):
        for c in range(paints):
            for mask in range(half):
                right_ensure(s, c, mask)
    for copy in right_exchange:
        copy.wait_send()
    for copy in right_copies.values():
        copy.wait_send()
    for away_from_here, copy in left_copies:
        @pl.when(away_from_here)
        def _():
            copy.wait_send()

    def right_dots(g):
        total = None
        for c in range(channels):
            source = lax.rem(g + shift_ref[c], NQ)
            term = lax.dot_general(
                mixed[c, source], right[c, g], (((1,), (1,)), ((), ())),
                preferred_element_type=jnp.float32,
            )
            total = term if total is None else total + term
        return total

    own_half = DP // ops * some * rows

    @pl.loop(0, NQ)
    def _(g):
        for c in range(channels):
            for u in range(bonds // 2):
                pair = [gathered[2 * u + t, c, g].astype(jnp.float32) for t in range(2)]
                for m in range(NPB):
                    at = m * B + u * sub
                    right[c, g, at:at + sub] = jnp.concatenate(
                        [x[m * fine:(m + 1) * fine] for x in pair], 0).astype(jnp.bfloat16)
        total = right_dots(g)
        for e in range(ops):
            part_sum[g, e] = total[e * own_half:(e + 1) * own_half]
        remote(part_sum.at[g, other], got_first.at[g], osend.at[g], orecv.at[g], bond, other).start()

    span = NB // streams

    def spot_of(s, m):
        return (s // span * NPB + m) * span + lax.rem(s, span)

    def view_second(j, c, s):
        return psi.at[j, o, c, :, pl.ds(s * NPB * span, NPB * span)]

    pl.semaphore_wait(free_sem, bits + 1)

    @pl.loop(0, NQ)
    def _(g):
        remote(part_sum.at[g, other], got_first.at[g], osend.at[g], orecv.at[g], bond, other).wait()
        total = (part_sum[g, o] + got_first[g]).astype(jnp.bfloat16)
        for p in range(DP // ops):
            for k in range(some):
                for m in range(NPB):
                    at = ((p * some + k) * NPB + m) * sub
                    for n in range(NPB):
                        psi[i, o, k, p, spot_of(g * NPB + n, m)] = total[at:at + sub, n * B:(n + 1) * B]

    unused, again_step, again_arrive, again_finish = spread(view_second, [], [turns, turns])
    for n in range(bits):
        again_step(0, n)
        again_step(1, n)
    again_arrive(0)

    def slot_of(x):
        return lax.rem(2 * x, half) + (2 * x) // half if not isinstance(x, int) else (2 * x) % half + (2 * x) // half

    def fetch_second(q, g, n):
        per = DP // ops
        return jnp.concatenate([
            jnp.concatenate([
                psi[slot_of(x), q // per, k, q % per, spot_of(g * NPB + n, m)]
                for m in range(NPB) for x in range(half)
            ], 0) for k in range(some)
        ], 1)

    holder = turn(i)
    trades = []

    def start_trade(s):
        wanted = psi.at[holder, o, :, :, pl.ds(s * NPB * span + (1 - part) * span, span)]
        trades.append(remote(wanted, swap.at[s], wsend.at[s], wrecv.at[s], partner, o))
        trades[-1].start()

    start_trade(0)
    left_dots(fetch_second, 0, NQ // streams)
    again_finish()
    start_trade(1)
    left_dots(fetch_second, NQ // streams, NQ // streams)

    @pl.loop(0, NQ)
    def _(g):
        total = right_dots(g)
        for x in range(DP * some):
            for m in range(NPB):
                at = x * rows + m * sub
                part_sum[g, m, x * sub:(x + 1) * sub] = total[at:at + sub]
        remote(part_sum.at[g, other], got_second.at[g], osend2.at[g], orecv2.at[g], bond, other).start()

    @pl.loop(0, NQ)
    def _(g):
        remote(part_sum.at[g, other], got_second.at[g], osend2.at[g], orecv2.at[g], bond, other).wait()
        total = (part_sum[g, o] + got_second[g]).astype(jnp.bfloat16)
        for n in range(NPB):
            for x in range(DP * some):
                sorted_out[g * NPB + n, x] = total[x * sub:(x + 1) * sub, n * B:(n + 1) * B]

    for r in range(NB):
        s = rank_ref[r]
        for p in range(DP):
            for k in range(some):
                ready[p * (NB // groups) + r // groups, k, r % groups] = sorted_out[s, p * some + k]

    sends = []
    for e in range(1, bonds):
        target = lax.rem(bond + e, bonds)
        copy = remote(ready.at[target], landed.at[bond], asend.at[e], arecv.at[e], target, o)
        copy.start()
        sends.append(copy)

    for copy in trades:
        copy.wait()
    for p in range(DP // ops):
        for r in range(NB):
            s = rank_ref[r]
            for k in range(some):
                cols = slice((p * NB + r) * B, (p * NB + r + 1) * B)
                one_ref[part * some + k, :, cols] = psi[
                    holder, o, k, p, spot_of(s, part)].astype(jnp.float32)
                one_ref[(1 - part) * some + k, :, cols] = swap[s // span, k, p, lax.rem(s, span)].astype(jnp.float32)

    landed[bond] = ready[bond]
    for copy in sends:
        copy.wait()
    for s in range(bonds):
        x = s % half
        spot = x // 2 + (x % 2) * (half // 2)
        for k in range(some):
            for at in range(groups):
                two_ref[(s // half) * some + k, spot * sub:(spot + 1) * sub, at * B:(at + 1) * B] = (
                    landed[s, k, at].astype(jnp.float32))


def whole(wave, left_tiles, right_tiles, tables, bonds, ops):
    roots, sector_rows, strip = wave.shape
    channels = left_tiles.shape[0]
    half = bonds // 2
    bits = half.bit_length() - 1
    some = roots // 2
    fine = left_tiles.shape[3]
    sub = 2 * fine
    rows = NPB * sub
    share = sector_rows // ops
    groups = strip // B
    height = DP * some * rows
    paints = 4
    vmem = pl.BlockSpec(memory_space=pltpu.VMEM)
    smem = pl.BlockSpec(memory_space=pltpu.SMEM)
    dma = pltpu.SemaphoreType.DMA
    bf, f32 = jnp.bfloat16, jnp.float32
    return pl.pallas_call(
        functools.partial(whole_kernel, half, ops, some, channels, site_charge_table),
        out_shape=[
            jax.ShapeDtypeStruct((roots, NPB * B // bonds, DP // ops * NB * B), f32),
            jax.ShapeDtypeStruct((roots, share, strip), f32),
        ],
        in_specs=[smem] * 4 + [pl.BlockSpec(memory_space=pl.ANY), vmem, vmem],
        out_specs=[vmem, vmem],
        scratch_shapes=[pltpu.SMEM((NB,), jnp.int32)] * 4 + [pltpu.SMEM((channels,), jnp.int32)] * 2 + [
            pltpu.SMEM((channels * DP * DP,), f32),
            pltpu.VMEM((half, ops, some, 2, groups * share // sub, sub, B), bf),
            pltpu.VMEM((bonds, channels, NQ, NPB * fine, NPB * B), bf),
            pltpu.VMEM((channels, NQ, NPB * B, NPB * B), bf),
            pltpu.VMEM((NQ, channels * rows, NPB * B), bf),
            pltpu.VMEM((2,) + left_tiles.shape, bf),
            pltpu.VMEM((channels, NQ, height, NPB * B), bf),
            pltpu.VMEM((NQ, ops, height // ops, NPB * B), f32),
            pltpu.VMEM((NQ, height // ops, NPB * B), f32),
            pltpu.VMEM((NQ, height // ops, NPB * B), f32),
            pltpu.VMEM((roots, share, strip), f32),
            pltpu.VMEM((some, groups * share // sub, sub, B), bf),
            pltpu.VMEM((2, some, DP // ops, NB // 2, sub, B), bf),
            pltpu.VMEM((NB, DP * some, sub, B), bf),
            pltpu.VMEM((bonds, some, groups, sub, B), bf),
            pltpu.VMEM((bonds, some, groups, sub, B), bf),
            dma, dma((some,)), dma((some,)),
            dma((2, some, half)), dma((2, some, half)), dma((2, some, half)), dma((2, some, half)),
            dma((paints,)), dma((paints,)), dma((2, paints, half)), dma((2, paints, half)),
            dma((2, paints)), dma((2, paints)), dma((paints,)),
            dma((NQ,)), dma((NQ,)), dma((NQ,)), dma((NQ,)),
            dma((2,)), dma((2,)), dma((bonds,)), dma((bonds,)),
            pltpu.SemaphoreType.REGULAR,
        ],
        compiler_params=pltpu.CompilerParams(
            collective_id=3, has_side_effects=True, vmem_limit_bytes=67043328
        ),
        name="whole",
    )(*tables, wave, left_tiles, right_tiles)


def local_whole(
    wavefunction, left_tiles, right_tiles, site_operators, left_charge, right_charge, channel_charge
):
    tables = (left_charge, right_charge, channel_charge, site_operators)
    return tuple(whole(
        wavefunction, left_tiles, right_tiles, tables, lax.axis_size("bond"), lax.axis_size("op")
    ))


def fits(mesh, wavefunction, left_tiles):
    bonds, ops = mesh.shape["bond"], mesh.shape["op"]
    strip = wavefunction.shape[2] // bonds
    fine = left_tiles.shape[3] // bonds
    channels = left_tiles.shape[0] // ops
    return (
        ops == NPB and bonds == NB and strip % B == 0 and 2 * fine * (bonds // 2) == B
        and channels % 4 == 0 and NPB * fine == 16
    )


def local(
    wavefunction, left_tiles, right_tiles, site_operators, left_charge, right_charge, channel_charge
):
    bonds = lax.axis_size("bond")
    ops = lax.axis_size("op")
    bond = lax.axis_index("bond")
    op = lax.axis_index("op")
    roots, sector_rows, strip = wavefunction.shape
    channels = site_operators.shape[0]
    half = bonds // 2
    part = bond // half
    some = roots // 2
    chunk = left_tiles.shape[3]
    band = 2 * chunk
    rows = NPB * band
    held = -(-rows // 16) * 16
    width = min(strip, B)
    groups = strip // width
    own_charge = lax.dynamic_slice_in_dim(channel_charge, op * channels, channels, 0)
    left_order = jnp.argsort(left_charge, stable=True).astype(jnp.int32)
    right_order = jnp.argsort(right_charge, stable=True).astype(jnp.int32)
    shift = (own_charge[:, 0] + own_charge[:, 1]) % NQ
    site = site_masks(site_operators, own_charge).reshape(-1)

    right = right_tiles[:, right_order].transpose(0, 1, 3, 2, 4).reshape(
        channels, NB, chunk, NPB * B
    )
    right = lax.all_gather(right, "bond", axis=2, tiled=True).reshape(
        channels, NQ, NPB * B, NPB * B
    )

    even = [(b, b // 2 + (b % 2) * half) for b in range(bonds)]
    odd = [(b, b // 2 + (1 - b % 2) * half) for b in range(bonds)]
    one = lax.ppermute(left_tiles, "bond", even)
    two = lax.ppermute(left_tiles, "bond", odd)
    low = jnp.where(part == 0, one, two)
    high = jnp.where(part == 0, two, one)
    left = jnp.concatenate([low, high], axis=3)
    left_slots = ((jnp.arange(NQ)[:, None] + own_charge[None, :, 0]) % NQ)[:, :, None] * NPB + jnp.arange(NPB)
    left = left[jnp.arange(channels)[None, :, None], left_order[left_slots]]
    left = left.transpose(0, 1, 2, 4, 3, 5).reshape(NQ, channels, rows, NPB * B)
    left = jnp.pad(left, ((0, 0), (0, 0), (0, held - rows), (0, 0)))
    left = left.reshape(NQ, channels * held, NPB * B)

    share = sector_rows // ops
    psi = lax.dynamic_slice_in_dim(wavefunction, op * share, share, 1).astype(jnp.bfloat16)
    psi = psi.reshape(2, some, share, groups, width).transpose(0, 1, 3, 2, 4)
    kept = lax.dynamic_index_in_dim(psi, part, 0, keepdims=False)
    other = lax.dynamic_index_in_dim(psi, 1 - part, 0, keepdims=False)
    (psi,) = spread(kept, other, half, ops, True)

    def load_whole(ref, block):
        return ref[block]

    def load_first(ref, block):
        owner = block // groups
        t, j, at = owner // half, lax.rem(owner, half), lax.rem(block, groups)
        return jnp.concatenate(
            [jnp.concatenate([ref[j, o, t, k, at] for o in range(ops)], 0) for k in range(some)], 1
        )

    load = load_first
    if width < B:
        psi = psi.reshape(half, ops, 2, some, share, strip).transpose(2, 0, 5, 1, 4, 3)
        psi = psi.reshape(DP * NB, B, sector_rows, some).transpose(0, 2, 3, 1)
        psi = psi.reshape(DP * NB, sector_rows, some * B)
        load = load_whole
    elif share % 16:
        psi = psi.transpose(2, 0, 4, 1, 5, 3, 6).reshape(DP * NB, sector_rows, some * B)
        load = load_whole

    def unpack(result):
        result = result.reshape(NB, DP, some, held, B)[:, :, :, :rows]
        return result.reshape(NB, DP, some, NPB, band, B)

    def summed_share(parts, axis):
        size = parts.shape[axis] // ops
        total = lax.dynamic_slice_in_dim(parts, op * size, size, axis)
        for e in range(1, ops):
            to = (op + e) % ops
            sent = lax.dynamic_slice_in_dim(parts, to * size, size, axis)
            total += lax.ppermute(sent, "op", [(o, (o + e) % ops) for o in range(ops)])
        return total

    first = unpack(apply_all(right_order, shift, site, psi, left, right, held, some, load))
    turned = (DP * NB, some, NPB, band, B)
    if DP % ops == 0:
        first = summed_share(first, 1).transpose(1, 0, 2, 3, 4, 5)
        first = first.reshape((DP * NB // ops,) + turned[1:])
    else:
        first = summed_share(first.transpose(1, 0, 2, 3, 4, 5).reshape(turned), 0)
    blocks = first.shape[0]

    mine = lax.dynamic_index_in_dim(first, part, 2, keepdims=False)
    theirs = lax.dynamic_index_in_dim(first, 1 - part, 2, keepdims=False)
    again = first.astype(jnp.bfloat16).transpose(1, 0, 2, 3, 4)
    again, back = spread(again, theirs.astype(jnp.bfloat16), half, ops, False)
    back = back.astype(jnp.float32)
    both = jnp.stack([jnp.where(part == 0, mine, back), jnp.where(part == 0, back, mine)])
    sigma_one = both.transpose(0, 2, 3, 1, 4).reshape(roots, band, blocks * B)

    def load_second(ref, block):
        o, at = block // blocks, lax.rem(block, blocks)
        return jnp.concatenate(
            [
                jnp.concatenate([ref[j, o, 0, k, at, m] for m in range(NPB) for j in range(half)], 0)
                for k in range(some)
            ], 1,
        )

    load = load_second
    if band % 16:
        again = again[:, :, 0].transpose(1, 3, 4, 0, 5, 2, 6)
        again = again.reshape(DP * NB, sector_rows, some * B)
        load = load_whole
    second = unpack(apply_all(right_order, shift, site, again, left, right, held, some, load))
    if ops == NPB:
        second = summed_share(second, 3)
    else:
        second = lax.psum(second, "op")
    tiles = second.shape[3]
    second = second.astype(jnp.bfloat16).transpose(2, 3, 4, 1, 0, 5)
    second = second.reshape(some, tiles * band, bonds, strip).transpose(2, 0, 1, 3)
    second = lax.all_to_all(second, "bond", split_axis=0, concat_axis=0, tiled=True)
    second = second.reshape(2, half, some, tiles, band, strip).transpose(0, 2, 3, 1, 4, 5)
    second = second.reshape(roots, tiles * B, strip).astype(jnp.float32)
    if ops != NPB:
        second = lax.dynamic_slice_in_dim(second, op * share, share, 1)
    return (sigma_one, second)


def solution(mesh):
    def run(*args):
        body = local_whole if fits(mesh, args[0], args[1]) else local
        return jax.shard_map(
            body,
            mesh=mesh,
            in_specs=(
                P(None, None, "bond"),
                P("op", None, None, "bond", None),
                P("op", None, None, "bond", None),
                P("op", None, None),
                P(),
                P(),
                P(),
            ),
            out_specs=(P(None, "bond", "op"), P(None, "op", "bond")),
            check_vma=False,
        )(*args)

    return run
```
